32 devices in a mesh: section: 2 (over y), fsdp: 4 (over x, core), replica: 4 (over z).
Axes of the slice: x: 2, y: 2, z: 4, core: 2. Of those that a mesh axis runs over, the one named last changes fastest.
Arguments:
- inputs: bfloat16 [2, 4, 512, 768], P(None, 'replica', 'fsdp'), may hold values from -6 to 6
- segments: int32 [2, 4, 512], P(None, 'replica'), may hold values from 0 to 4, as said below
- cotangent: bfloat16 [2, 4, 512, 768], P(None, 'replica', 'fsdp'), may hold values from -6 to 6
- ln1_gain: bfloat16 [2, 768], P('section', 'fsdp'), may hold values from 0.5 to 1.5
- ln1_bias: bfloat16 [2, 768], P('section', 'fsdp'), may hold values from -3 to 3
- qkv_weight: bfloat16 [2, 768, 2304], P('section', 'fsdp'), may hold values from -0.21875 to 0.21875
- qv_bias: bfloat16 [2, 1536], P('section', 'fsdp'), may hold values from -3 to 3
- out_weight: bfloat16 [2, 768, 768], P('section', 'fsdp'), may hold values from -0.875 to 0.875
- out_bias: bfloat16 [2, 768], P('section', 'fsdp'), may hold values from -3 to 3
- ln2_gain: bfloat16 [2, 768], P('section', 'fsdp'), may hold values from 0.5 to 1.5
- ln2_bias: bfloat16 [2, 768], P('section', 'fsdp'), may hold values from -3 to 3
- up_weight: bfloat16 [2, 768, 3072], P('section', 'fsdp'), may hold values from -0.21875 to 0.21875
- up_bias: bfloat16 [2, 3072], P('section', 'fsdp'), may hold values from -3 to 3
- down_weight: bfloat16 [2, 3072, 768], P('section', 'fsdp'), may hold values from -0.109375 to 0.109375
- down_bias: bfloat16 [2, 768], P('section', 'fsdp'), may hold values from -3 to 3
Outputs:
- acts: bfloat16 [2, 2, 4, 512, 768], P('section', None, 'replica', 'fsdp')
- grads_in: float32 [2, 2, 4, 512, 768], P('section', None, 'replica', 'fsdp')
- ln1_gain_grad: float32 [2, 768], P('section', 'fsdp')
- ln1_bias_grad: float32 [2, 768], P('section', 'fsdp')
- qkv_weight_grad: float32 [2, 768, 2304], P('section', 'fsdp')
- qv_bias_grad: float32 [2, 1536], P('section', 'fsdp')
- out_weight_grad: float32 [2, 768, 768], P('section', 'fsdp')
- out_bias_grad: float32 [2, 768], P('section', 'fsdp')
- ln2_gain_grad: float32 [2, 768], P('section', 'fsdp')
- ln2_bias_grad: float32 [2, 768], P('section', 'fsdp')
- up_weight_grad: float32 [2, 768, 3072], P('section', 'fsdp')
- up_bias_grad: float32 [2, 3072], P('section', 'fsdp')
- down_weight_grad: float32 [2, 3072, 768], P('section', 'fsdp')
- down_bias_grad: float32 [2, 768], P('section', 'fsdp')
The draws below stay inside these ranges and needn't reach their ends.
Inputs may be any that keep to these rules, and one draw needn't show every extreme that they name: `segments`: along each sequence the numbers never fall and each of the five documents 0 to 4 is present; document 0 ends before position 128 and document 1 runs past position 384.
All inputs are finite; a program needn't handle non-finite values.
Results may differ from the reference program's by a relative error of at most 0.017.
Values may be sent and summed in bfloat16 or wider, within the bound.
No kernel may reach another device: no remote copies, remote signals or barrier semaphores. Data moves between devices by JAX's collectives and lax.ppermute only.
A program may use at most 192 MiB of HBM per device.

```python
import jax
import jax.numpy as jnp
from jax import lax

D = 768
HEADS = 12
HD = 64
FF = 3072
L = 512
MB = 2
NSEQ = 4


def draw_segments(key, part):
    key_list = jax.random.split(key, 4)
    shape = (MB, NSEQ, 1)
    first_end = jax.random.randint(key_list[0], shape, 1, L // 4, dtype=jnp.int32)
    second_end = jax.random.randint(key_list[1], shape, L * 13 // 16, L * 7 // 8 + 1, dtype=jnp.int32)
    third_end = jax.random.randint(key_list[2], shape, L * 29 // 32, L * 15 // 16 + 1, dtype=jnp.int32)
    fourth_end = jax.random.randint(key_list[3], shape, L * 31 // 32, L, dtype=jnp.int32)
    places = jnp.arange(L, dtype=jnp.int32)[None, None, :]
    numbers = (places >= first_end).astype(jnp.int32) + (places >= second_end).astype(jnp.int32)
    numbers = numbers + (places >= third_end).astype(jnp.int32) + (places >= fourth_end).astype(jnp.int32)
    return numbers


def steps_of(rng, shape, shards, least, largest):
    level = 1.0
    for dim, blocks in shards:
        steps = jax.random.uniform(jax.random.fold_in(jax.random.fold_in(rng, 6), dim), (blocks,), jnp.float32, least / len(shards), largest / len(shards))
        level = level * jnp.repeat(jnp.exp(steps), shape[dim] // blocks).reshape((-1,) + (1,) * (len(shape) - 1 - dim))
    return level


def normal_values(own_key, extent, deviation, reach, shards=(), held_as=jnp.bfloat16):
    values = deviation * jax.random.normal(own_key, extent, jnp.float32)
    if shards:
        values = values * steps_of(own_key, extent, shards, -0.22, 0.18)
    return jnp.clip(values, -reach, reach).astype(held_as)


def setup_inputs(seed: int = 0) -> dict:
    keys = jax.random.split(jax.random.key(seed), 16)
    return {
        "inputs": normal_values(keys[0], (MB, NSEQ, L, D), 1.0, 6.0, ((1, 4), (2, 4))),
        "segments": draw_segments(jax.random.fold_in(keys[15], 71), 0),
        "cotangent": normal_values(keys[2], (MB, NSEQ, L, D), 1.0, 6.0, ((1, 4), (2, 4))),
        "ln1_gain": jnp.clip(1.0 + 0.1 * jax.random.normal(keys[3], (2, D), jnp.float32), 0.5, 1.5).astype(jnp.bfloat16),
        "ln1_bias": normal_values(keys[4], (2, D), 0.3, 3.0, ((0, 2), (1, 4))),
        "qkv_weight": normal_values(keys[5], (2, D, 3 * D), D ** -0.5, 0.21875, ((0, 2), (1, 4))),
        "qv_bias": normal_values(keys[6], (2, 2 * D), 0.5, 3.0, ((0, 2), (1, 4))),
        "out_weight": normal_values(keys[7], (2, D, D), (D // 16) ** -0.5, 0.875, ((0, 2), (1, 4))),
        "out_bias": normal_values(keys[8], (2, D), 0.3, 3.0, ((0, 2), (1, 4))),
        "ln2_gain": jnp.clip(1.0 + 0.1 * jax.random.normal(keys[9], (2, D), jnp.float32), 0.5, 1.5).astype(jnp.bfloat16),
        "ln2_bias": normal_values(keys[10], (2, D), 0.3, 3.0, ((0, 2), (1, 4))),
        "up_weight": normal_values(keys[11], (2, D, FF), D ** -0.5, 0.21875, ((0, 2), (1, 4))),
        "up_bias": normal_values(keys[12], (2, FF), 0.5, 3.0, ((0, 2), (1, 4))),
        "down_weight": normal_values(keys[13], (2, FF, D), FF ** -0.5, 0.109375, ((0, 2), (1, 4))),
        "down_bias": normal_values(keys[14], (2, D), 0.3, 3.0, ((0, 2), (1, 4))),
    }


epsilon = 1e-05
masked_value = -1e+30
highest = lax.Precision.HIGHEST

@jax.custom_vjp
def low(v):
    return lax.optimization_barrier(v.astype(jnp.bfloat16)).astype(jnp.float32)

@jax.custom_vjp
def low_back(v):
    return v

def low_keep(v):
    return (low(v), None)

def low_pass(kept, grad):
    return (grad,)

def back_keep(v):
    return (v, None)

def back_low(kept, grad):
    return (low(grad),)
low.defvjp(low_keep, low_pass)
low_back.defvjp(back_keep, back_low)

def matmul(left, right):
    return jnp.dot(left, right, precision=highest, preferred_element_type=jnp.float32)

def layer_norm(values, gain, offset):
    centred = values - lax.optimization_barrier(jnp.mean(values, axis=-1, keepdims=True))
    inverse = lax.rsqrt(lax.optimization_barrier(jnp.mean(centred * centred, axis=-1, keepdims=True)) + epsilon)
    return centred * inverse * gain + offset

def attention(queries, key_rows, value_rows, segment_row):
    length = queries.shape[0]
    query_heads = queries.reshape(length, HEADS, HD)
    key_heads = key_rows.reshape(length, HEADS, HD)
    value_heads = value_rows.reshape(length, HEADS, HD)
    scores = jnp.einsum('qhd,khd->hqk', query_heads, key_heads, precision=highest) * HD ** (-0.5)
    scores = low_back(scores)
    places = jnp.arange(length, dtype=jnp.int32)
    allowed = (places[None, :] <= places[:, None]) & (segment_row[None, :] == segment_row[:, None])
    allowed = allowed[None]
    shifted = jnp.where(allowed, scores, masked_value)
    top_score = lax.optimization_barrier(jnp.max(shifted, axis=-1, keepdims=True))
    exp_scores = jnp.where(allowed, jnp.exp(shifted - top_score), 0.0)
    probs = low(exp_scores / lax.optimization_barrier(jnp.sum(exp_scores, axis=-1, keepdims=True)))
    mixed_rows = jnp.einsum('hqk,khd->qhd', probs, value_heads, precision=highest)
    return mixed_rows.reshape(length, D)

def layer(hidden_in, params, segment_row):
    gain_one, offset_one, qkv_full, qv_full, out_full, out_offset, gain_two, offset_two, up_full, up_offset, down_full, down_offset = params
    normed_one = low(layer_norm(hidden_in, gain_one, offset_one))
    bias_full = jnp.concatenate([qv_full[:D], jnp.zeros((D,), qv_full.dtype), qv_full[D:]])
    projected = low_back(low(matmul(normed_one, qkv_full) + bias_full))
    mixed_rows = low_back(low(attention(projected[:, :D], projected[:, D:2 * D], projected[:, 2 * D:], segment_row)))
    branch = low_back(matmul(mixed_rows, out_full) + out_offset)
    middle = hidden_in + branch
    normed_two = low(layer_norm(middle, gain_two, offset_two))
    pre_act = low_back(matmul(normed_two, up_full) + up_offset)
    activated = low(jax.nn.gelu(pre_act, approximate=True))
    return middle + low_back(matmul(activated, down_full) + down_offset)

def reference(inputs, segments, cotangent, ln1_gain, ln1_bias, qkv_weight, qv_bias, out_weight, out_bias, ln2_gain, ln2_bias, up_weight, up_bias, down_weight, down_bias):
    params_all = tuple((param.astype(jnp.float32) for param in (ln1_gain, ln1_bias, qkv_weight, qv_bias, out_weight, out_bias, ln2_gain, ln2_bias, up_weight, up_bias, down_weight, down_bias)))
    first_layer = tuple((param[0] for param in params_all))
    second_layer = tuple((param[1] for param in params_all))
    seq_total = MB * NSEQ
    flat_in = inputs.astype(jnp.float32).reshape(seq_total, L, D)
    flat_seg = segments.reshape(seq_total, L)
    flat_cot = cotangent.astype(jnp.float32).reshape(seq_total, L, D)
    zero_grads = tuple((jnp.zeros_like(param) for param in first_layer))

    def per_sequence(grad_carry, seq_items):
        grads_one, grads_two = grad_carry
        row_in, segment_row, row_cot = seq_items

        def run_layer(hidden_in, params):
            return layer(hidden_in, params, segment_row)
        out_one, back_one = jax.vjp(run_layer, row_in, first_layer)
        passed = low(out_one)
        out_two, back_two = jax.vjp(run_layer, passed, second_layer)
        grad_mid, param_two = back_two(row_cot)
        grad_first, param_one = back_one(low(grad_mid))
        grads_one = jax.tree.map(jnp.add, grads_one, param_one)
        grads_two = jax.tree.map(jnp.add, grads_two, param_two)
        return ((grads_one, grads_two), (out_one.astype(jnp.bfloat16), out_two.astype(jnp.bfloat16), grad_first, grad_mid))
    (sums_one, sums_two), (acts_one, acts_two, grad_first, grad_mid) = lax.scan(per_sequence, (zero_grads, zero_grads), (flat_in, flat_seg, flat_cot))
    acts = jnp.stack([acts_one, acts_two]).reshape(2, MB, NSEQ, L, D)
    grads_in = jnp.stack([grad_first, grad_mid]).reshape(2, MB, NSEQ, L, D)
    stacked = tuple((jnp.stack([first_sum, second_sum]) for first_sum, second_sum in zip(sums_one, sums_two)))
    return (acts, grads_in, stacked[0], stacked[1], stacked[2], stacked[3], stacked[4], stacked[5], stacked[6], stacked[7], stacked[8], stacked[9], stacked[10], stacked[11])
```

```python
import jax
import jax.numpy as jnp
from jax import lax
from jax.sharding import PartitionSpec as P

HEADS = 12
HD = 64
EPS = 1e-05
MASKED = -1e30
F32 = jnp.float32
BF16 = jnp.bfloat16


def across(value):
    return lax.ppermute(value, "fsdp", [(i, i ^ 2) for i in range(4)])


def between(value):
    return lax.ppermute(value, "fsdp", [(i, i ^ 1) for i in range(4)])


def ordered(place, own, other, axis=0):
    first = place == 0
    return jnp.stack([jnp.where(first, own, other), jnp.where(first, other, own)], axis)


def pick(value, place, axis=0):
    return lax.dynamic_index_in_dim(value, place, axis, keepdims=False)


def matmul(left, right):
    return jnp.dot(left, right, preferred_element_type=F32)


def matmul_t(left, right):
    return lax.dot_general(left, right, (((1,), (1,)), ((), ())), preferred_element_type=F32)


def t_matmul(left, right):
    return lax.dot_general(left, right, (((0,), (0,)), ((), ())), preferred_element_type=F32)


def normalised(values):
    centred = values - jnp.mean(values, axis=-1, keepdims=True)
    inverse = lax.rsqrt(jnp.mean(centred * centred, axis=-1, keepdims=True) + EPS)
    return centred * inverse, inverse


def norm_back(grad, xhat, inverse, gain):
    scaled = grad * gain
    return inverse * (
        scaled
        - jnp.mean(scaled, axis=-1, keepdims=True)
        - xhat * jnp.mean(scaled * xhat, axis=-1, keepdims=True)
    )


def gelu_parts(u):
    a = 0.7978845608028654
    b = 0.044715
    t = jnp.tanh(a * (u + b * u * u * u))
    value = 0.5 * u * (1.0 + t)
    slope = 0.5 * (1.0 + t) + 0.5 * u * (1.0 - t * t) * a * (1.0 + 3.0 * b * u * u)
    return value, slope


def attend(hidden, allowed, w):
    xhat, inverse = normalised(hidden.astype(F32))
    normed = (xhat * w["ln1_gain"] + w["ln1_bias"]).astype(BF16)
    rows = hidden.shape[0]
    width = w["qkv"].shape[1] // 3
    qkv = (matmul(normed, w["qkv"]) + w["qkv_bias"]).astype(BF16)
    q, k, v = (qkv[:, i * width : (i + 1) * width].reshape(rows, -1, HD) for i in range(3))
    scores = jnp.einsum("qhd,khd->hqk", q, k, preferred_element_type=F32) * HD**-0.5
    shifted = jnp.where(allowed, scores, MASKED)
    top = jnp.max(shifted, axis=-1, keepdims=True)
    exps = jnp.where(allowed, jnp.exp(shifted - top), 0.0)
    probs = exps / jnp.sum(exps, axis=-1, keepdims=True)
    mixed = jnp.einsum("hqk,khd->qhd", probs.astype(BF16), v, preferred_element_type=F32)
    mixed = mixed.reshape(rows, width).astype(BF16)
    part = matmul(mixed, w["out"]).astype(BF16)
    return part, (normed, qkv, probs.astype(BF16), mixed)


def feed(middle, w):
    xhat, inverse = normalised(middle)
    normed = (xhat * w["ln2_gain"] + w["ln2_bias"]).astype(BF16)
    pre = matmul(normed, w["up"]) + w["up_bias"]
    value, slope = gelu_parts(pre)
    activated = value.astype(BF16)
    part = matmul(activated, w["down"])
    return part, (normed, activated, slope.astype(BF16))


def forward(hidden, allowed, w, core):
    part, attn_state = attend(hidden, allowed, w)
    middle = hidden.astype(F32) + part.astype(F32) + between(part).astype(F32) + w["out_bias"]
    part, feed_state = feed(middle, w)
    blocks = part.reshape(2, 2, -1, part.shape[-1])
    own = pick(blocks, core, 1)
    other = between(pick(blocks, 1 - core, 1).astype(BF16))
    own_middle = pick(middle.reshape(blocks.shape), core, 1)
    result = own_middle + own + other.astype(F32) + w["down_bias"]
    return result.astype(BF16), (middle, attn_state, feed_state)


def feed_back(grad, state, w):
    normed, activated, slope = state
    g_act = matmul_t(grad, w["down"])
    g_pre = (g_act * slope.astype(F32)).astype(BF16)
    part = matmul_t(g_pre, w["up"]).astype(BF16)
    return g_pre, part


def attend_back(g_branch, state, w):
    normed, qkv, probs, mixed = state
    rows = qkv.shape[0]
    width = qkv.shape[1] // 3
    scale = HD**-0.5
    q, k, v = (qkv[:, i * width : (i + 1) * width].reshape(rows, -1, HD) for i in range(3))
    g_mixed = matmul_t(g_branch, w["out"]).astype(BF16).reshape(rows, -1, HD)
    g_probs = jnp.einsum("qhd,khd->hqk", g_mixed, v, preferred_element_type=F32)
    p = probs.astype(F32)
    inner = jnp.sum(p * g_probs, axis=-1, keepdims=True)
    g_scores = (p * (g_probs - inner)).astype(BF16)
    g_q = jnp.einsum("hqk,khd->qhd", g_scores, k, preferred_element_type=F32) * scale
    g_k = jnp.einsum("hqk,qhd->khd", g_scores, q, preferred_element_type=F32) * scale
    g_v = jnp.einsum("hqk,qhd->khd", probs, g_mixed, preferred_element_type=F32)
    g_qkv = jnp.concatenate([g.reshape(rows, width).astype(BF16) for g in (g_q, g_k, g_v)], axis=1)
    part = matmul_t(g_qkv, w["qkv"]).astype(BF16)
    return g_qkv, part


def backward(grad, hidden, state, w, core):
    middle, attn_state, feed_state = state
    g_pre, part = feed_back(grad, feed_state, w)
    g_norm2 = part.astype(F32) + between(part).astype(F32)
    xhat2, inv2 = normalised(middle)
    g_middle = grad.astype(F32) + norm_back(g_norm2, xhat2, inv2, w["ln2_gain"])
    g_branch = g_middle.astype(BF16)
    g_qkv, part = attend_back(g_branch, attn_state, w)
    shape = (2, 2, -1, part.shape[-1])
    blocks = part.reshape(shape)
    g_norm1 = pick(blocks, core, 1).astype(F32) + between(pick(blocks, 1 - core, 1)).astype(F32)
    xhat1, inv1 = normalised(pick(hidden.reshape(shape), core, 1).astype(F32))
    own_middle = pick(g_middle.reshape(shape), core, 1)
    g_input = own_middle + norm_back(g_norm1, xhat1, inv1, w["ln1_gain"])
    return g_input, (g_pre, g_norm2, xhat2, g_branch, g_qkv, g_norm1, xhat1)


def line_sum(value):
    size = lax.axis_size("replica")
    if size != 4:
        return lax.psum(value.astype(F32), "replica")
    kind = value.dtype
    place = lax.axis_index("replica")

    def add(a, b):
        return (a.astype(F32) + b.astype(F32)).astype(kind)

    inward = lax.ppermute(value, "replica", [(0, 1), (3, 2)])
    half = add(value, inward)
    total = add(half, lax.ppermute(half, "replica", [(1, 2), (2, 1)]))
    outward = lax.ppermute(total, "replica", [(1, 0), (2, 3)])
    return jnp.where((place == 0) | (place == 3), outward, total).astype(F32)


def shards(
    inputs,
    segments,
    cotangent,
    ln1_gain,
    ln1_bias,
    qkv_weight,
    qv_bias,
    out_weight,
    out_bias,
    ln2_gain,
    ln2_bias,
    up_weight,
    up_bias,
    down_weight,
    down_bias,
):
    place = lax.axis_index("fsdp")
    chip, core = place // 2, place % 2
    is_first = lax.axis_index("section") == 0
    width = inputs.shape[-1]
    half = width // 2
    shard = width // 4
    hidden_units = up_weight.shape[-1]
    group = hidden_units // 4

    def both(rows):
        return ordered(core, rows, between(rows), 1).reshape(-1, width)

    def entered(values):
        mine = pick(values, chip, 0)[0]
        other = across(pick(values, 1 - chip, 0)[0])
        return both(ordered(chip, mine, other))

    small = jnp.concatenate(
        [v[0] for v in (ln1_gain, ln1_bias, qv_bias, out_bias, ln2_gain, ln2_bias, up_bias, down_bias)]
    )
    pair = ordered(core, small, between(small))
    small = ordered(chip, pair, across(pair)).reshape(4, -1).astype(F32)
    sizes = [shard, shard, 2 * shard, shard, shard, shard, group, shard]
    vectors = []
    at = 0
    for size in sizes:
        vectors.append(small[:, at : at + size].reshape(-1))
        at += size
    hidden = entered(inputs)

    qkv_halves = qkv_weight[0].reshape(shard, 3, 2, half)
    own = pick(qkv_halves, core, 2)
    rows = ordered(core, own, between(pick(qkv_halves, 1 - core, 2)))
    qkv = ordered(chip, rows, across(rows)).reshape(width, 3 * half)

    out = ordered(chip, out_weight[0], across(out_weight[0]))
    out = ordered(core, pick(out, core), between(pick(out, 1 - core))).reshape(half, width)

    up_groups = up_weight[0].reshape(shard, 2, 2, group)
    own = pick(up_groups, core, 2)
    rows = ordered(core, own, between(pick(up_groups, 1 - core, 2)))
    up = ordered(chip, rows, across(rows)).reshape(width, 2 * group)
    down = ordered(chip, down_weight[0], across(down_weight[0])).reshape(2 * group, width)

    qv = vectors[2].reshape(2, 2, half)
    zeros = jnp.zeros((half,), F32)
    w = {
        "ln1_gain": vectors[0],
        "ln1_bias": vectors[1],
        "qkv": qkv,
        "qkv_bias": jnp.concatenate([pick(qv[0], core), zeros, pick(qv[1], core)]),
        "out": out,
        "out_bias": vectors[3],
        "ln2_gain": vectors[4],
        "ln2_bias": vectors[5],
        "up": up,
        "up_bias": pick(vectors[6].reshape(2, 2, group), core, 1).reshape(-1),
        "down": down,
        "down_bias": vectors[7],
    }
    segment = pick(segments, chip, 0)[0]
    length = segment.shape[0]
    at = jnp.arange(length, dtype=jnp.int32)
    allowed = ((at[None, :] <= at[:, None]) & (segment[None, :] == segment[:, None]))[None]

    result, _ = forward(hidden, allowed, w, core)
    arrived = both(lax.ppermute(result, "section", [(0, 1)]))
    hidden = jnp.where(is_first, hidden, arrived)
    result, state = forward(hidden, allowed, w, core)

    grad = entered(cotangent)
    g_input, _ = backward(grad, hidden, state, w, core)
    arrived = both(lax.ppermute(g_input.astype(BF16), "section", [(1, 0)]))
    grad = jnp.where(is_first, arrived, grad)
    g_input, terms = backward(grad, hidden, state, w, core)
    g_pre, g_norm2, xhat2, g_branch, g_qkv, g_norm1, xhat1 = terms
    middle, (normed1, _, _, mixed), (normed2, activated, _) = state

    def shared(value, axis=0):
        mine = pick(value, chip, axis)
        other = across(pick(value, 1 - chip, axis).astype(BF16))
        return mine + other.astype(F32)

    def swapped(value):
        mine = pick(value, core).astype(BF16)
        other = between(pick(value, 1 - core).astype(BF16))
        return mine, other

    down_grad = shared(t_matmul(activated, grad).reshape(2, group, width)).astype(BF16)
    down_grad = jnp.concatenate([line_sum(p) for p in jnp.split(down_grad, 2)])

    up_term = shared(t_matmul(normed2, g_pre).reshape(2, 2 * shard, 2 * group))
    mine, other = swapped(up_term.reshape(2, shard, 2, group))
    up_grad = ordered(core, mine, other, 2).reshape(shard, hidden_units)
    up_grad = jnp.concatenate([line_sum(p) for p in jnp.split(up_grad, 2)])

    out_term = t_matmul(mixed, g_branch).astype(BF16).reshape(2, shard, width)
    out_term = ordered(core, pick(out_term, core), between(pick(out_term, 1 - core)))
    out_grad = line_sum(shared(out_term.astype(F32)).astype(BF16))

    qkv_term = shared(t_matmul(normed1, g_qkv).reshape(2, 2 * shard, 3 * half))
    mine, other = swapped(qkv_term.reshape(2, shard, 3, half))
    qkv_grad = ordered(core, mine, other, 2).reshape(shard, 3 * width)
    qkv_grad = jnp.concatenate([line_sum(p) for p in jnp.split(qkv_grad, 2)])

    def once(value):
        return jnp.where(core == 0, value, 0.0)

    def placed_half(value):
        return ordered(core, value, jnp.zeros_like(value))

    bias_sums = jnp.sum(g_qkv.astype(F32), axis=0).reshape(3, half)
    qv_grad = jnp.concatenate([placed_half(bias_sums[0]), placed_half(bias_sums[2])])
    up_sums = jnp.sum(g_pre.astype(F32), axis=0).reshape(2, group)
    up_bias_grad = ordered(core, up_sums, jnp.zeros_like(up_sums), 1)
    small_grads = [
        jnp.sum(g_norm1 * xhat1, axis=(0, 1)),
        jnp.sum(g_norm1, axis=(0, 1)),
        qv_grad,
        once(jnp.sum(g_branch.astype(F32), axis=0)),
        once(jnp.sum(g_norm2 * xhat2, axis=0)),
        once(jnp.sum(g_norm2, axis=0)),
        up_bias_grad,
        once(jnp.sum(grad.astype(F32), axis=0)),
    ]
    small_grads = jnp.concatenate([v.reshape(2, 2, -1) for v in small_grads], axis=-1)
    small_grads = pick(small_grads, core, 1) + between(pick(small_grads, 1 - core, 1))
    small_grads = pick(small_grads, chip) + across(pick(small_grads, 1 - chip))
    small_grads = line_sum(small_grads)
    small_out = []
    at = 0
    for size in sizes:
        small_out.append(small_grads[None, at : at + size])
        at += size
    g_ln1g, g_ln1b, g_qv, g_outb, g_ln2g, g_ln2b, g_upb, g_downb = small_out

    def left(value, wire):
        mine = pick(value, chip)
        other = across(pick(value, 1 - chip).astype(wire)).astype(value.dtype)
        return ordered(chip, mine, other)[None, :, None]

    acts = left(result, BF16)
    grads_in = left(g_input, BF16)
    return (
        acts,
        grads_in,
        g_ln1g,
        g_ln1b,
        qkv_grad[None],
        g_qv,
        out_grad[None],
        g_outb,
        g_ln2g,
        g_ln2b,
        up_grad[None],
        g_upb,
        down_grad[None],
        g_downb,
    )


def solution(mesh):
    rows = P(None, "replica", "fsdp", None)
    vector = P("section", "fsdp")
    matrix = P("section", "fsdp", None)
    layer = P("section", None, "replica", "fsdp", None)
    weights = (
        vector,
        vector,
        matrix,
        vector,
        matrix,
        vector,
        vector,
        vector,
        matrix,
        vector,
        matrix,
        vector,
    )
    return jax.shard_map(
        shards,
        mesh=mesh,
        in_specs=(rows, P(None, "replica", None), rows) + weights,
        out_specs=(layer, layer) + weights,
        check_vma=False,
    )
```

```python
import jax
import jax.numpy as jnp
from jax import lax
from jax.sharding import PartitionSpec as P

HEADS = 12
HD = 64
EPS = 1e-05
MASKED = -1e30
F32 = jnp.float32
BF16 = jnp.bfloat16


def across(value):
    return lax.ppermute(value, "fsdp", [(i, i ^ 2) for i in range(4)])


def between(value):
    return lax.ppermute(value, "fsdp", [(i, i ^ 1) for i in range(4)])


def ordered(place, own, other, axis=0):
    first = place == 0
    return jnp.stack([jnp.where(first, own, other), jnp.where(first, other, own)], axis)


def pick(value, place, axis=0):
    return lax.dynamic_index_in_dim(value, place, axis, keepdims=False)


def matmul(left, right):
    return jnp.dot(left, right, preferred_element_type=F32)


def matmul_t(left, right):
    return lax.dot_general(left, right, (((1,), (1,)), ((), ())), preferred_element_type=F32)


def t_matmul(left, right):
    return lax.dot_general(left, right, (((0,), (0,)), ((), ())), preferred_element_type=F32)


def normalised(values):
    centred = values - jnp.mean(values, axis=-1, keepdims=True)
    inverse = lax.rsqrt(jnp.mean(centred * centred, axis=-1, keepdims=True) + EPS)
    return centred * inverse, inverse


def norm_back(grad, xhat, inverse, gain):
    scaled = grad * gain
    return inverse * (
        scaled
        - jnp.mean(scaled, axis=-1, keepdims=True)
        - xhat * jnp.mean(scaled * xhat, axis=-1, keepdims=True)
    )


def gelu_parts(u):
    a = 0.7978845608028654
    b = 0.044715
    t = jnp.tanh(a * (u + b * u * u * u))
    value = 0.5 * u * (1.0 + t)
    slope = 0.5 * (1.0 + t) + 0.5 * u * (1.0 - t * t) * a * (1.0 + 3.0 * b * u * u)
    return value, slope


def attend(hidden, allowed, w):
    xhat, inverse = normalised(hidden.astype(F32))
    normed = (xhat * w["ln1_gain"] + w["ln1_bias"]).astype(BF16)
    rows = hidden.shape[0]
    width = w["qkv"].shape[1] // 3
    qkv = (matmul(normed, w["qkv"]) + w["qkv_bias"]).astype(BF16)
    q, k, v = (qkv[:, i * width : (i + 1) * width].reshape(rows, -1, HD) for i in range(3))
    scores = jnp.einsum("qhd,khd->hqk", q, k, preferred_element_type=F32) * HD**-0.5
    shifted = jnp.where(allowed, scores, MASKED)
    top = jnp.max(shifted, axis=-1, keepdims=True)
    exps = jnp.where(allowed, jnp.exp(shifted - top), 0.0)
    probs = exps / jnp.sum(exps, axis=-1, keepdims=True)
    mixed = jnp.einsum("hqk,khd->qhd", probs.astype(BF16), v, preferred_element_type=F32)
    mixed = mixed.reshape(rows, width).astype(BF16)
    part = matmul(mixed, w["out"]).astype(BF16)
    return part, (normed, qkv, probs.astype(BF16), mixed)


def feed(middle, w):
    xhat, inverse = normalised(middle)
    normed = (xhat * w["ln2_gain"] + w["ln2_bias"]).astype(BF16)
    pre = matmul(normed, w["up"]) + w["up_bias"]
    value, slope = gelu_parts(pre)
    activated = value.astype(BF16)
    part = matmul(activated, w["down"])
    return part, (normed, activated, slope.astype(BF16))


def forward(hidden, allowed, w, core):
    part, attn_state = attend(hidden, allowed, w)
    middle = hidden.astype(F32) + part.astype(F32) + between(part).astype(F32) + w["out_bias"]
    part, feed_state = feed(middle, w)
    blocks = part.reshape(2, 2, -1, part.shape[-1])
    own = pick(blocks, core, 1)
    other = between(pick(blocks, 1 - core, 1).astype(BF16))
    own_middle = pick(middle.reshape(blocks.shape), core, 1)
    result = own_middle + own + other.astype(F32) + w["down_bias"]
    return result.astype(BF16), (middle, attn_state, feed_state)


def feed_back(grad, state, w):
    normed, activated, slope = state
    g_act = matmul_t(grad, w["down"])
    g_pre = (g_act * slope.astype(F32)).astype(BF16)
    part = matmul_t(g_pre, w["up"]).astype(BF16)
    return g_pre, part


def attend_back(g_branch, state, w):
    normed, qkv, probs, mixed = state
    rows = qkv.shape[0]
    width = qkv.shape[1] // 3
    scale = HD**-0.5
    q, k, v = (qkv[:, i * width : (i + 1) * width].reshape(rows, -1, HD) for i in range(3))
    g_mixed = matmul_t(g_branch, w["out"]).astype(BF16).reshape(rows, -1, HD)
    g_probs = jnp.einsum("qhd,khd->hqk", g_mixed, v, preferred_element_type=F32)
    p = probs.astype(F32)
    inner = jnp.sum(p * g_probs, axis=-1, keepdims=True)
    g_scores = (p * (g_probs - inner)).astype(BF16)
    g_q = jnp.einsum("hqk,khd->qhd", g_scores, k, preferred_element_type=F32) * scale
    g_k = jnp.einsum("hqk,qhd->khd", g_scores, q, preferred_element_type=F32) * scale
    g_v = jnp.einsum("hqk,qhd->khd", probs, g_mixed, preferred_element_type=F32)
    g_qkv = jnp.concatenate([g.reshape(rows, width).astype(BF16) for g in (g_q, g_k, g_v)], axis=1)
    part = matmul_t(g_qkv, w["qkv"]).astype(BF16)
    return g_qkv, part


def backward(grad, hidden, state, w, core):
    middle, attn_state, feed_state = state
    g_pre, part = feed_back(grad, feed_state, w)
    g_norm2 = part.astype(F32) + between(part).astype(F32)
    xhat2, inv2 = normalised(middle)
    g_middle = grad.astype(F32) + norm_back(g_norm2, xhat2, inv2, w["ln2_gain"])
    g_branch = g_middle.astype(BF16)
    g_qkv, part = attend_back(g_branch, attn_state, w)
    shape = (2, 2, -1, part.shape[-1])
    blocks = part.reshape(shape)
    g_norm1 = pick(blocks, core, 1).astype(F32) + between(pick(blocks, 1 - core, 1)).astype(F32)
    xhat1, inv1 = normalised(pick(hidden.reshape(shape), core, 1).astype(F32))
    own_middle = pick(g_middle.reshape(shape), core, 1)
    g_input = own_middle + norm_back(g_norm1, xhat1, inv1, w["ln1_gain"])
    return g_input, (g_pre, g_norm2, xhat2, g_branch, g_qkv, g_norm1, xhat1)


def line_sum(value):
    size = lax.axis_size("replica")
    if size != 4:
        return lax.psum(value.astype(F32), "replica")
    place = lax.axis_index("replica")
    half = value + lax.ppermute(value, "replica", [(0, 1), (3, 2)])
    total = half + lax.ppermute(half, "replica", [(1, 2), (2, 1)])
    outward = lax.ppermute(total, "replica", [(1, 0), (2, 3)])
    return jnp.where((place == 0) | (place == 3), outward, total)


class LineSum:
    LAG = 3

    def __init__(self):
        self.size = lax.axis_size("replica")
        place = lax.axis_index("replica")
        self.outer = (place == 0) | (place == 3)
        self.units, self.halves, self.totals, self.results = [], [], [], []

    def add(self, a, b):
        return (a.astype(F32) + b.astype(F32)).astype(BF16)

    def put(self, unit):
        self.step(unit)

    def step(self, unit):
        if self.size != 4:
            if unit is not None:
                self.results.append(lax.psum(unit.astype(F32), "replica"))
            return
        back = len(self.units) - self.LAG
        self.units.append(unit)
        if back < 0:
            got = lax.ppermute(unit, "replica", [(0, 1), (3, 2)])
        elif unit is None:
            got = lax.ppermute(self.totals[back], "replica", [(1, 0), (2, 3)])
        else:
            sent = jnp.where(self.outer, unit, self.totals[back])
            got = lax.ppermute(sent, "replica", [(0, 1), (1, 0), (2, 3), (3, 2)])
        if back >= 0:
            self.results.append(jnp.where(self.outer, got, self.totals[back]).astype(F32))
        if unit is not None:
            half = self.add(unit, got)
            self.halves.append(half)
            middle = lax.ppermute(half, "replica", [(1, 2), (2, 1)])
            self.totals.append(self.add(half, middle))

    def finish(self):
        for _ in range(self.LAG):
            self.step(None)
        return self.results


def tied(value, *others):
    return lax.optimization_barrier((value,) + others)[0]


def shards(
    inputs,
    segments,
    cotangent,
    ln1_gain,
    ln1_bias,
    qkv_weight,
    qv_bias,
    out_weight,
    out_bias,
    ln2_gain,
    ln2_bias,
    up_weight,
    up_bias,
    down_weight,
    down_bias,
):
    place = lax.axis_index("fsdp")
    chip, core = place // 2, place % 2
    is_first = lax.axis_index("section") == 0
    width = inputs.shape[-1]
    half = width // 2
    shard = width // 4
    hidden_units = up_weight.shape[-1]
    group = hidden_units // 4

    def both(rows):
        return ordered(core, rows, between(rows), 1).reshape(-1, width)

    def entered(values):
        mine = pick(values, chip, 0)[0]
        other = across(pick(values, 1 - chip, 0)[0])
        return both(ordered(chip, mine, other))

    small = jnp.concatenate(
        [v[0] for v in (ln1_gain, ln1_bias, qv_bias, out_bias, ln2_gain, ln2_bias, up_bias, down_bias)]
    )
    pair = ordered(core, small, between(small))
    small = ordered(chip, pair, across(pair)).reshape(4, -1).astype(F32)
    sizes = [shard, shard, 2 * shard, shard, shard, shard, group, shard]
    vectors = []
    at = 0
    for size in sizes:
        vectors.append(small[:, at : at + size].reshape(-1))
        at += size
    hidden = entered(inputs)

    qkv_halves = qkv_weight[0].reshape(shard, 3, 2, half)
    own = pick(qkv_halves, core, 2)
    rows = ordered(core, own, between(pick(qkv_halves, 1 - core, 2)))
    qkv = ordered(chip, rows, across(rows)).reshape(width, 3 * half)

    out = ordered(chip, out_weight[0], across(out_weight[0]))
    out = ordered(core, pick(out, core), between(pick(out, 1 - core))).reshape(half, width)

    up_groups = up_weight[0].reshape(shard, 2, 2, group)
    own = pick(up_groups, core, 2)
    rows = ordered(core, own, between(pick(up_groups, 1 - core, 2)))
    up = ordered(chip, rows, across(rows)).reshape(width, 2 * group)
    down = ordered(chip, down_weight[0], across(down_weight[0])).reshape(2 * group, width)

    qv = vectors[2].reshape(2, 2, half)
    zeros = jnp.zeros((half,), F32)
    w = {
        "ln1_gain": vectors[0],
        "ln1_bias": vectors[1],
        "qkv": qkv,
        "qkv_bias": jnp.concatenate([pick(qv[0], core), zeros, pick(qv[1], core)]),
        "out": out,
        "out_bias": vectors[3],
        "ln2_gain": vectors[4],
        "ln2_bias": vectors[5],
        "up": up,
        "up_bias": pick(vectors[6].reshape(2, 2, group), core, 1).reshape(-1),
        "down": down,
        "down_bias": vectors[7],
    }
    segment = pick(segments, chip, 0)[0]
    length = segment.shape[0]
    at = jnp.arange(length, dtype=jnp.int32)
    allowed = ((at[None, :] <= at[:, None]) & (segment[None, :] == segment[:, None]))[None]

    result, _ = forward(hidden, allowed, w, core)
    arrived = both(lax.ppermute(result, "section", [(0, 1)]))
    hidden = jnp.where(is_first, hidden, arrived)
    result, state = forward(hidden, allowed, w, core)

    grad = entered(cotangent)
    g_input, _ = backward(grad, hidden, state, w, core)
    arrived = both(lax.ppermute(g_input.astype(BF16), "section", [(1, 0)]))
    grad = jnp.where(is_first, arrived, grad)
    middle, attn_state, feed_state = state
    normed1, qkv_rows, probs, mixed = attn_state
    normed2, activated, slope = feed_state
    line = LineSum()

    def shared(mine, other):
        return (mine + across(other.astype(BF16)).astype(F32)).astype(BF16)

    term = t_matmul(activated, grad).reshape(2, 4, shard, width)
    mine, other = pick(term, chip), pick(term, 1 - chip)
    units = [shared(mine[i], other[i]) for i in range(4)]

    g_act = matmul_t(grad, w["down"])
    g_pre = (g_act * slope.astype(F32)).astype(BF16)
    term = t_matmul(normed2, g_pre).reshape(2, 2, shard, 2, group)
    mine, other = pick(term, chip), pick(term, 1 - chip)
    for i in range(2):
        sums = shared(mine[:, :, i], other[:, :, i])
        units += [pick(sums, core), between(pick(sums, 1 - core))]

    part = matmul_t(g_pre, w["up"]).astype(BF16)
    g_norm2 = part.astype(F32) + between(part).astype(F32)
    xhat2, inv2 = normalised(middle)
    g_middle = grad.astype(F32) + norm_back(g_norm2, xhat2, inv2, w["ln2_gain"])
    g_branch = tied(g_middle.astype(BF16), units[0])
    line.put(units[0])
    line.put(units[1])

    rows = qkv_rows.shape[0]
    scale = HD**-0.5
    q, k, v = (qkv_rows[:, i * half : (i + 1) * half].reshape(rows, -1, HD) for i in range(3))
    g_mixed = matmul_t(g_branch, w["out"]).astype(BF16).reshape(rows, -1, HD)
    g_probs = jnp.einsum("qhd,khd->hqk", g_mixed, v, preferred_element_type=F32)
    p = probs.astype(F32)
    inner = jnp.sum(p * g_probs, axis=-1, keepdims=True)
    g_scores = (p * (g_probs - inner)).astype(BF16)
    g_scores = tied(g_scores, *line.halves[:1])
    g_q = jnp.einsum("hqk,khd->qhd", g_scores, k, preferred_element_type=F32) * scale
    g_k = jnp.einsum("hqk,qhd->khd", g_scores, q, preferred_element_type=F32) * scale
    g_v = jnp.einsum("hqk,qhd->khd", probs, g_mixed, preferred_element_type=F32)
    g_qkv = jnp.concatenate([g.reshape(rows, half).astype(BF16) for g in (g_q, g_k, g_v)], axis=1)
    g_qkv = tied(g_qkv, *line.halves[1:2])

    term = t_matmul(mixed, g_branch).astype(BF16).reshape(2, shard, width)
    term = ordered(core, pick(term, core), between(pick(term, 1 - core)))
    units.append(shared(pick(term, chip).astype(F32), pick(term, 1 - chip)))

    term = t_matmul(normed1, g_qkv).reshape(2, 2, shard, 3, half)
    mine, other = pick(term, chip), pick(term, 1 - chip)
    for i in range(3):
        sums = shared(mine[:, :, i], other[:, :, i])
        units.append(jnp.concatenate([pick(sums, core), between(pick(sums, 1 - core))], axis=1))

    part = matmul_t(g_qkv, w["qkv"]).astype(BF16)
    block_shape = (2, 2, -1, width)
    blocks = part.reshape(block_shape)
    g_norm1 = pick(blocks, core, 1).astype(F32) + between(pick(blocks, 1 - core, 1)).astype(F32)
    xhat1, inv1 = normalised(pick(hidden.reshape(block_shape), core, 1).astype(F32))
    own_middle = pick(g_middle.reshape(block_shape), core, 1)
    g_input = own_middle + norm_back(g_norm1, xhat1, inv1, w["ln1_gain"])

    for unit in units[2:]:
        line.put(unit)
    done = line.finish()
    down_grad = jnp.concatenate(done[:4])
    up_grad = jnp.stack([ordered(core, done[4 + 2 * i], done[5 + 2 * i], 1) for i in range(2)], axis=1)
    up_grad = up_grad.reshape(shard, hidden_units)
    out_grad = done[8]
    qkv_grad = [ordered(core, done[9 + i][:, :half], done[9 + i][:, half:], 1) for i in range(3)]
    qkv_grad = jnp.stack(qkv_grad, axis=1).reshape(shard, 3 * width)

    def once(value):
        return jnp.where(core == 0, value, 0.0)

    def placed_half(value):
        return ordered(core, value, jnp.zeros_like(value))

    bias_sums = jnp.sum(g_qkv.astype(F32), axis=0).reshape(3, half)
    qv_grad = jnp.concatenate([placed_half(bias_sums[0]), placed_half(bias_sums[2])])
    up_sums = jnp.sum(g_pre.astype(F32), axis=0).reshape(2, group)
    up_bias_grad = ordered(core, up_sums, jnp.zeros_like(up_sums), 1)
    small_grads = [
        jnp.sum(g_norm1 * xhat1, axis=(0, 1)),
        jnp.sum(g_norm1, axis=(0, 1)),
        qv_grad,
        once(jnp.sum(g_branch.astype(F32), axis=0)),
        once(jnp.sum(g_norm2 * xhat2, axis=0)),
        once(jnp.sum(g_norm2, axis=0)),
        up_bias_grad,
        once(jnp.sum(grad.astype(F32), axis=0)),
    ]
    small_grads = jnp.concatenate([v.reshape(2, 2, -1) for v in small_grads], axis=-1)
    small_grads = pick(small_grads, core, 1) + between(pick(small_grads, 1 - core, 1))
    small_grads = pick(small_grads, chip) + across(pick(small_grads, 1 - chip))
    small_grads = line_sum(small_grads)
    small_out = []
    at = 0
    for size in sizes:
        small_out.append(small_grads[None, at : at + size])
        at += size
    g_ln1g, g_ln1b, g_qv, g_outb, g_ln2g, g_ln2b, g_upb, g_downb = small_out

    def left(value, wire):
        mine = pick(value, chip)
        other = across(pick(value, 1 - chip).astype(wire)).astype(value.dtype)
        return ordered(chip, mine, other)[None, :, None]

    acts = left(result, BF16)
    grads_in = left(g_input, BF16)
    return (
        acts,
        grads_in,
        g_ln1g,
        g_ln1b,
        qkv_grad[None],
        g_qv,
        out_grad[None],
        g_outb,
        g_ln2g,
        g_ln2b,
        up_grad[None],
        g_upb,
        down_grad[None],
        g_downb,
    )


def solution(mesh):
    rows = P(None, "replica", "fsdp", None)
    vector = P("section", "fsdp")
    matrix = P("section", "fsdp", None)
    layer = P("section", None, "replica", "fsdp", None)
    weights = (
        vector,
        vector,
        matrix,
        vector,
        matrix,
        vector,
        vector,
        vector,
        matrix,
        vector,
        matrix,
        vector,
    )
    return jax.shard_map(
        shards,
        mesh=mesh,
        in_specs=(rows, P(None, "replica", None), rows) + weights,
        out_specs=(layer, layer) + weights,
        check_vma=False,
    )
```

```python
import jax
import jax.numpy as jnp
from jax import lax
from jax.sharding import PartitionSpec as P

HEADS = 12
HD = 64
EPS = 1e-05
MASKED = -1e30
F32 = jnp.float32
BF16 = jnp.bfloat16


def across(value):
    return lax.ppermute(value, "fsdp", [(i, i ^ 2) for i in range(4)])


def between(value):
    return lax.ppermute(value, "fsdp", [(i, i ^ 1) for i in range(4)])


def ordered(place, own, other, axis=0):
    first = place == 0
    return jnp.stack([jnp.where(first, own, other), jnp.where(first, other, own)], axis)


def joined(place, own, other, axis=0):
    first = place == 0
    return jnp.concatenate([jnp.where(first, own, other), jnp.where(first, other, own)], axis)


def part_of(value, place, size, axis=0):
    return lax.dynamic_slice_in_dim(value, place * size, size, axis)


def pick(value, place, axis=0):
    return lax.dynamic_index_in_dim(value, place, axis, keepdims=False)


def matmul(left, right):
    return jnp.dot(left, right, preferred_element_type=F32)


def matmul_t(left, right):
    return lax.dot_general(left, right, (((1,), (1,)), ((), ())), preferred_element_type=F32)


def t_matmul(left, right):
    return lax.dot_general(left, right, (((0,), (0,)), ((), ())), preferred_element_type=F32)


def normalised(values):
    centred = values - jnp.mean(values, axis=-1, keepdims=True)
    inverse = lax.rsqrt(jnp.mean(centred * centred, axis=-1, keepdims=True) + EPS)
    return centred * inverse, inverse


def norm_back(grad, xhat, inverse, gain):
    scaled = grad * gain
    return inverse * (
        scaled
        - jnp.mean(scaled, axis=-1, keepdims=True)
        - xhat * jnp.mean(scaled * xhat, axis=-1, keepdims=True)
    )


def gelu_parts(u):
    a = 0.7978845608028654
    b = 0.044715
    t = jnp.tanh(a * (u + b * u * u * u))
    value = 0.5 * u * (1.0 + t)
    slope = 0.5 * (1.0 + t) + 0.5 * u * (1.0 - t * t) * a * (1.0 + 3.0 * b * u * u)
    return value, slope


def attend(hidden, allowed, w):
    xhat, inverse = normalised(hidden.astype(F32))
    normed = (xhat * w["ln1_gain"] + w["ln1_bias"]).astype(BF16)
    rows = hidden.shape[0]
    width = w["qkv"].shape[1] // 3
    qkv = (matmul(normed, w["qkv"]) + w["qkv_bias"]).astype(BF16)
    q, k, v = (qkv[:, i * width : (i + 1) * width].reshape(rows, -1, HD) for i in range(3))
    scores = jnp.einsum("qhd,khd->hqk", q, k, preferred_element_type=F32) * HD**-0.5
    shifted = jnp.where(allowed, scores, MASKED)
    top = jnp.max(shifted, axis=-1, keepdims=True)
    exps = jnp.where(allowed, jnp.exp(shifted - top), 0.0)
    probs = exps / jnp.sum(exps, axis=-1, keepdims=True)
    mixed = jnp.einsum("hqk,khd->qhd", probs.astype(BF16), v, preferred_element_type=F32)
    mixed = mixed.reshape(rows, width).astype(BF16)
    part = matmul(mixed, w["out"]).astype(BF16)
    return part, (normed, qkv, probs.astype(BF16), mixed)


def feed(middle, w):
    xhat, inverse = normalised(middle)
    normed = (xhat * w["ln2_gain"] + w["ln2_bias"]).astype(BF16)
    activated, slopes = [], []
    part = None
    for up, bias, down in zip(w["up"], w["up_bias"], w["down"]):
        value, slope = gelu_parts(matmul(normed, up) + bias)
        value, slope = lax.optimization_barrier((value.astype(BF16), slope.astype(BF16)))
        activated.append(value)
        slopes.append(slope)
        term = matmul(value, down)
        part = term if part is None else part + term
    return part, (normed, activated, slopes)


def forward(hidden, allowed, w, core):
    part, attn_state = attend(hidden, allowed, w)
    middle = hidden.astype(F32) + part.astype(F32) + between(part).astype(F32) + w["out_bias"]
    part, feed_state = feed(middle, w)
    rows = part.shape[0] // 2
    other = between(part_of(part, 1 - core, rows).astype(BF16))
    result = part_of(middle, core, rows) + part_of(part, core, rows) + other.astype(F32) + w["down_bias"]
    return result.astype(BF16), (middle, attn_state, feed_state)


def feed_back(grad, slopes, w):
    g_pre = []
    part = None
    for slope, up, down in zip(slopes, w["up"], w["down"]):
        g = (matmul_t(grad, down) * slope.astype(F32)).astype(BF16)
        g_pre.append(g)
        term = matmul_t(g, up)
        part = term if part is None else part + term
    return g_pre, part.astype(BF16)


def attend_back(g_branch, state, w):
    normed, qkv, probs, mixed = state
    rows = qkv.shape[0]
    width = qkv.shape[1] // 3
    scale = HD**-0.5
    q, k, v = (qkv[:, i * width : (i + 1) * width].reshape(rows, -1, HD) for i in range(3))
    g_mixed = matmul_t(g_branch, w["out"]).astype(BF16).reshape(rows, -1, HD)
    g_probs = jnp.einsum("qhd,khd->hqk", g_mixed, v, preferred_element_type=F32)
    p = probs.astype(F32)
    inner = jnp.sum(p * g_probs, axis=-1, keepdims=True)
    g_scores = (p * (g_probs - inner)).astype(BF16)
    g_q = jnp.einsum("hqk,khd->qhd", g_scores, k, preferred_element_type=F32) * scale
    g_k = jnp.einsum("hqk,qhd->khd", g_scores, q, preferred_element_type=F32) * scale
    g_v = jnp.einsum("hqk,qhd->khd", probs, g_mixed, preferred_element_type=F32)
    g_qkv = jnp.concatenate([g.reshape(rows, width).astype(BF16) for g in (g_q, g_k, g_v)], axis=1)
    part = matmul_t(g_qkv, w["qkv"]).astype(BF16)
    return g_qkv, part


def middle_back(part, grad, middle, w):
    g_norm2 = part.astype(F32) + between(part).astype(F32)
    xhat2, inv2 = normalised(middle)
    g_middle = grad.astype(F32) + norm_back(g_norm2, xhat2, inv2, w["ln2_gain"])
    return g_middle, g_norm2, xhat2


def input_back(part, hidden, g_middle, w, core):
    rows = part.shape[0] // 2
    g_norm1 = part_of(part, core, rows).astype(F32) + between(part_of(part, 1 - core, rows)).astype(F32)
    xhat1, inv1 = normalised(part_of(hidden, core, rows).astype(F32))
    own_middle = part_of(g_middle, core, rows)
    return own_middle + norm_back(g_norm1, xhat1, inv1, w["ln1_gain"]), g_norm1, xhat1


def tied(value, *others):
    return lax.optimization_barrier((value,) + others)[0]


class Sums:
    HOPS = ([(0, 1), (3, 2)], [(1, 2), (2, 1)], [(1, 0), (2, 3)])

    def __init__(self, count):
        self.line = lax.axis_size("replica") == 4
        place = lax.axis_index("replica")
        self.outer = (place == 0) | (place == 3)
        self.values = {}
        self.results = {}
        self.last = None
        stages = 4 if self.line else 1
        self.events = sorted((p + s, -s, p) for p in range(count) for s in range(stages))

    def chained(self, value):
        if self.last is not None:
            value = tied(value, self.last)
        self.last = value
        return value

    def put(self, piece, mine, other, after=None):
        self.values[piece] = (mine, across(other.astype(BF16)), after)

    def run(self, until=None):
        while self.events:
            _, stage, piece = self.events.pop(0)
            stage = -stage
            if stage == 0:
                mine, got, after = self.values[piece]
                value = (mine.astype(F32) + self.chained(got).astype(F32)).astype(BF16)
                value = value if after is None else after(value)
                if not self.line:
                    self.results[piece] = lax.psum(value.astype(F32), "replica")
            else:
                value, got = self.values[piece]
                got = self.chained(got)
                if stage == 3:
                    self.results[piece] = jnp.where(self.outer, got, value).astype(F32)
                else:
                    value = (value.astype(F32) + got.astype(F32)).astype(BF16)
            if self.line and stage < 3:
                self.values[piece] = (value, lax.ppermute(value, "replica", self.HOPS[stage]))
            if until == (piece, stage):
                break
        return self.last


def shards(
    inputs,
    segments,
    cotangent,
    ln1_gain,
    ln1_bias,
    qkv_weight,
    qv_bias,
    out_weight,
    out_bias,
    ln2_gain,
    ln2_bias,
    up_weight,
    up_bias,
    down_weight,
    down_bias,
):
    place = lax.axis_index("fsdp")
    chip, core = place // 2, place % 2
    is_first = lax.axis_index("section") == 0
    width = inputs.shape[-1]
    half = width // 2
    shard = width // 4
    hidden_units = up_weight.shape[-1]
    group = hidden_units // 4

    def both(rows):
        return joined(core, rows, between(rows))

    def entered(values):
        mine = pick(values, chip, 0)[0]
        other = across(pick(values, 1 - chip, 0)[0])
        pair = ordered(chip, mine, other)
        return ordered(core, pair, between(pair), 1).reshape(-1, width), other

    small = jnp.concatenate(
        [v[0] for v in (ln1_gain, ln1_bias, qv_bias, out_bias, ln2_gain, ln2_bias, up_bias, down_bias)]
    )
    pair = ordered(core, small, between(small))
    small = ordered(chip, pair, across(pair)).reshape(4, -1).astype(F32)
    sizes = [shard, shard, 2 * shard, shard, shard, shard, group, shard]
    vectors = []
    at = 0
    for size in sizes:
        vectors.append(small[:, at : at + size].reshape(-1))
        at += size
    hidden, first = entered(inputs)

    def rows_of(value, size):
        count = value.shape[1] // (2 * size)
        sides = [
            jnp.concatenate([part_of(value, 2 * i + place, size, 1) for i in range(count)], 1)
            for place in (core, 1 - core)
        ]
        return joined(core, sides[0], between(sides[1]))

    own_qkv = rows_of(qkv_weight[0], half)
    got_qkv = across(qkv_weight[0])
    qkv = joined(chip, own_qkv, rows_of(got_qkv, half))

    got_out = tied(across(tied(out_weight[0], first)), got_qkv)
    same = chip == core
    out = joined(
        core,
        jnp.where(same, out_weight[0], got_out),
        between(jnp.where(same, got_out, out_weight[0])),
    )

    own, other = (part_of(up_weight[0], place, 2 * group, 1) for place in (chip, 1 - chip))
    got_up = tied(across(tied(other, first)), got_out)
    got_other = tied(across(tied(own, got_qkv)), got_up)
    got_down = tied(across(tied(down_weight[0][: group // 2], got_out)), got_other)
    got_last = tied(across(tied(down_weight[0][group // 2 :], got_up)), got_down)
    own, other = rows_of(own, group), rows_of(other, group)
    up = [
        joined(chip, own, rows_of(got_up, group)),
        joined(chip, other, rows_of(got_other, group)),
    ]
    down = [down_weight[0], jnp.concatenate([got_down, got_last])]

    qv = vectors[2].reshape(2, 2, half)
    zeros = jnp.zeros((half,), F32)
    up_vector = pick(vectors[6].reshape(2, 2, group), core, 1)
    w = {
        "ln1_gain": vectors[0],
        "ln1_bias": vectors[1],
        "qkv": qkv,
        "qkv_bias": jnp.concatenate([pick(qv[0], core), zeros, pick(qv[1], core)]),
        "out": out,
        "out_bias": vectors[3],
        "ln2_gain": vectors[4],
        "ln2_bias": vectors[5],
        "up": up,
        "up_bias": [pick(up_vector, chip), pick(up_vector, 1 - chip)],
        "down": down,
        "down_bias": vectors[7],
    }
    segment = pick(segments, chip, 0)[0]
    length = segment.shape[0]
    at = jnp.arange(length, dtype=jnp.int32)
    allowed = ((at[None, :] <= at[:, None]) & (segment[None, :] == segment[:, None]))[None]

    result, _ = forward(hidden, allowed, w, core)
    arrived = both(lax.ppermute(result, "section", [(0, 1)]))
    grad, _ = entered(tied(cotangent, result))
    hidden = jnp.where(is_first, hidden, arrived)
    result, state = forward(hidden, allowed, w, core)
    middle, attn_state, (normed2, activated, slopes) = state
    normed1, qkv_rows, probs, mixed = attn_state

    g_pre, part = feed_back(grad, slopes, w)
    g_middle, _, _ = middle_back(part, grad, middle, w)
    g_qkv, part = attend_back(g_middle.astype(BF16), attn_state, w)
    g_input, _, _ = input_back(part, hidden, g_middle, w, core)

    def left(value):
        block = value.shape[0] // 2
        pair = ordered(core, part_of(value, core, block), between(part_of(value, 1 - core, block)))
        return ordered(chip, pick(pair, chip), across(pick(pair, 1 - chip)))[None, :, None]

    arrived = both(lax.ppermute(g_input.astype(BF16), "section", [(1, 0)]))
    acts = left(tied(result, g_input))
    grad = jnp.where(is_first, arrived, grad)

    sums = Sums(6)
    rows = hidden.shape[0]

    def sides(values):
        return tuple(part_of(values, place, half, 1) for place in (chip, 1 - chip))

    def swapped(value):
        return jnp.concatenate([part_of(value, core, shard), between(part_of(value, 1 - core, shard))])

    other = t_matmul(activated[1], grad).astype(BF16)
    mine = t_matmul(activated[0], grad)
    for i in range(2):
        at = slice(i * group // 2, (i + 1) * group // 2)
        sums.put(i, mine[at], other[at])
    g_pre, part = feed_back(grad, slopes, w)
    stay, leave = sides(normed2)
    for i in range(2):
        other = t_matmul(leave, g_pre[1 - i]).astype(BF16)
        mine = t_matmul(stay, g_pre[i])
        sums.put(2 + i, mine, other, swapped)
    g_middle, g_norm2, xhat2 = middle_back(part, grad, middle, w)
    g_branch = tied(g_middle.astype(BF16), sums.run((0, 0)))
    g_qkv, part = attend_back(g_branch, attn_state, w)
    g_qkv = tied(g_qkv, sums.run((1, 0)))

    stay, leave = sides(normed1)
    sums.put(4, t_matmul(stay, g_qkv[:, :width]), t_matmul(leave, g_qkv[:, :width]).astype(BF16), swapped)
    term = t_matmul(mixed, g_branch).astype(BF16)
    term = joined(core, part_of(term, core, shard), between(part_of(term, 1 - core, shard)))

    def folded(value):
        return jnp.concatenate([value[:, :half], value[:, half:]])

    stay = jnp.concatenate(
        [t_matmul(stay, g_qkv[:, width:]), folded(part_of(term, chip, shard)).astype(F32)], 1
    )
    leave = jnp.concatenate(
        [t_matmul(leave, g_qkv[:, width:]).astype(BF16), folded(part_of(term, 1 - chip, shard))], 1
    )
    g_input, g_norm1, xhat1 = input_back(part, hidden, g_middle, w, core)

    def once(value):
        return jnp.where(core == 0, value, 0.0)

    def placed_half(value):
        return ordered(core, value, jnp.zeros_like(value))

    bias_sums = jnp.sum(g_qkv.astype(F32), axis=0).reshape(3, half)
    qv_grad = jnp.concatenate([placed_half(bias_sums[0]), placed_half(bias_sums[2])])
    up_sums = ordered(chip, *(jnp.sum(g.astype(F32), axis=0) for g in g_pre))
    up_bias_grad = ordered(core, up_sums, jnp.zeros_like(up_sums), 1)
    small_grads = [
        jnp.sum(g_norm1 * xhat1, axis=0),
        jnp.sum(g_norm1, axis=0),
        qv_grad,
        once(jnp.sum(g_branch.astype(F32), axis=0)),
        once(jnp.sum(g_norm2 * xhat2, axis=0)),
        once(jnp.sum(g_norm2, axis=0)),
        up_bias_grad,
        once(jnp.sum(grad.astype(F32), axis=0)),
    ]
    small_grads = jnp.concatenate([v.reshape(2, 2, -1) for v in small_grads], axis=-1)
    small_grads = pick(small_grads, core, 1) + between(pick(small_grads, 1 - core, 1))
    small_grads = small_grads.reshape(2, 3, width)
    sums.put(
        5,
        jnp.concatenate([stay, pick(small_grads, chip)]),
        jnp.concatenate([leave, pick(small_grads, 1 - chip).astype(BF16)]),
        lambda v: jnp.concatenate(
            [jnp.concatenate([swapped(v[: 2 * shard, :half]), v[: 2 * shard, half:]], 1), v[2 * shard :]]
        ),
    )
    grads_in = left(g_input.astype(BF16)).astype(F32)
    sums.run()
    done = sums.results
    down_grad = jnp.concatenate([done[0], done[1]])
    up_grad = joined(chip, *(joined(core, done[2 + i][:shard], done[2 + i][shard:], 1) for i in range(2)), 1)
    query_key, value_out, small_grads = done[4], done[5][: 2 * shard], done[5][2 * shard :].reshape(-1)
    qkv_grad = [
        joined(core, u[:shard], u[shard:], 1)
        for u in (query_key[:, :half], query_key[:, half:], value_out[:, :half])
    ]
    qkv_grad = jnp.concatenate(qkv_grad, 1)
    out_grad = jnp.concatenate([value_out[:shard, half:], value_out[shard:, half:]], 1)
    small_out = []
    at = 0
    for size in sizes:
        small_out.append(small_grads[None, at : at + size])
        at += size
    g_ln1g, g_ln1b, g_qv, g_outb, g_ln2g, g_ln2b, g_upb, g_downb = small_out
    return (
        acts,
        grads_in,
        g_ln1g,
        g_ln1b,
        qkv_grad[None],
        g_qv,
        out_grad[None],
        g_outb,
        g_ln2g,
        g_ln2b,
        up_grad[None],
        g_upb,
        down_grad[None],
        g_downb,
    )


def solution(mesh):
    rows = P(None, "replica", "fsdp", None)
    vector = P("section", "fsdp")
    matrix = P("section", "fsdp", None)
    layer = P("section", None, "replica", "fsdp", None)
    weights = (
        vector,
        vector,
        matrix,
        vector,
        matrix,
        vector,
        vector,
        vector,
        matrix,
        vector,
        matrix,
        vector,
    )
    return jax.shard_map(
        shards,
        mesh=mesh,
        in_specs=(rows, P(None, "replica", None), rows) + weights,
        out_specs=(layer, layer) + weights,
        check_vma=False,
    )
```

```python
import jax
import jax.numpy as jnp
from jax import lax
from jax.experimental import pallas as pl
from jax.experimental.pallas import tpu as pltpu
from jax.sharding import PartitionSpec as P

HEADS = 12
HD = 64
EPS = 1e-05
MASKED = -1e30
F32 = jnp.float32
BF16 = jnp.bfloat16
ROWS = 128


def across(value):
    return lax.ppermute(value, "fsdp", [(i, i ^ 2) for i in range(4)])


def between(value):
    return lax.ppermute(value, "fsdp", [(i, i ^ 1) for i in range(4)])


def ordered(place, own, other, axis=0):
    first = place == 0
    return jnp.stack([jnp.where(first, own, other), jnp.where(first, other, own)], axis)


def joined(place, own, other, axis=0):
    first = place == 0
    return jnp.concatenate([jnp.where(first, own, other), jnp.where(first, other, own)], axis)


def part_of(value, place, size, axis=0):
    return lax.dynamic_slice_in_dim(value, place * size, size, axis)


def pick(value, place, axis=0):
    return lax.dynamic_index_in_dim(value, place, axis, keepdims=False)


def matmul(left, right):
    return jnp.dot(left, right, preferred_element_type=F32)


def matmul_t(left, right):
    return lax.dot_general(left, right, (((1,), (1,)), ((), ())), preferred_element_type=F32)


def t_matmul(left, right):
    return lax.dot_general(left, right, (((0,), (0,)), ((), ())), preferred_element_type=F32)


def normalised(values):
    centred = values - jnp.mean(values, axis=-1, keepdims=True)
    inverse = lax.rsqrt(jnp.mean(centred * centred, axis=-1, keepdims=True) + EPS)
    return centred * inverse, inverse


def norm_back(grad, xhat, inverse, gain):
    scaled = grad * gain
    return inverse * (
        scaled
        - jnp.mean(scaled, axis=-1, keepdims=True)
        - xhat * jnp.mean(scaled * xhat, axis=-1, keepdims=True)
    )


def gelu_parts(u):
    a = 0.7978845608028654
    b = 0.044715
    t = jnp.tanh(a * (u + b * u * u * u))
    value = 0.5 * u * (1.0 + t)
    slope = 0.5 * (1.0 + t) + 0.5 * u * (1.0 - t * t) * a * (1.0 + 3.0 * b * u * u)
    return value, slope


def feed(middle, w):
    xhat, inverse = normalised(middle)
    normed = (xhat * w["ln2_gain"] + w["ln2_bias"]).astype(BF16)
    activated, slopes = [], []
    part = None
    for up, bias, down in zip(w["up"], w["up_bias"], w["down"]):
        value, slope = gelu_parts(matmul(normed, up) + bias)
        value, slope = lax.optimization_barrier((value.astype(BF16), slope.astype(BF16)))
        activated.append(value)
        slopes.append(slope)
        term = matmul(value, down)
        part = term if part is None else part + term
    return part, (normed, activated, slopes)


def forward(hidden, attention, w, core):
    part, *attn_state = attention(hidden)
    middle = hidden.astype(F32) + part.astype(F32) + between(part).astype(F32) + w["out_bias"]
    part, feed_state = feed(middle, w)
    rows = part.shape[0] // 2
    other = between(part_of(part, 1 - core, rows).astype(BF16))
    result = part_of(middle, core, rows) + part_of(part, core, rows) + other.astype(F32) + w["down_bias"]
    return result.astype(BF16), (middle, attn_state, feed_state)


def feed_back(grad, slopes, w):
    g_pre = []
    part = None
    for slope, up, down in zip(slopes, w["up"], w["down"]):
        g = (matmul_t(grad, down) * slope.astype(F32)).astype(BF16)
        g_pre.append(g)
        term = matmul_t(g, up)
        part = term if part is None else part + term
    return g_pre, part.astype(BF16)


def call(kernel, outs, scratch, args, flops, smem=()):
    spec = pl.BlockSpec(memory_space=pltpu.VMEM)
    moved = sum(a.size * a.dtype.itemsize for a in args)
    moved += sum(o.size * o.dtype.itemsize for o in outs)
    return pl.pallas_call(
        kernel,
        out_shape=tuple(outs),
        in_specs=[pl.BlockSpec(memory_space=pltpu.SMEM) if i in smem else spec for i in range(len(args))],
        out_specs=tuple(spec for _ in outs),
        scratch_shapes=scratch,
        compiler_params=pltpu.CompilerParams(vmem_limit_bytes=40 << 20),
        cost_estimate=pl.CostEstimate(flops=flops, bytes_accessed=moved, transcendentals=0),
    )(*args)


def shape(dims, kind):
    return jax.ShapeDtypeStruct(dims, kind)


def split_heads(pair):
    lane = lax.broadcasted_iota(jnp.int32, pair.shape, 1)
    zero = jnp.zeros_like(pair)
    return jnp.concatenate([jnp.where(lane < HD, pair, zero), jnp.where(lane < HD, zero, pair)], axis=0)


def join_heads(stacked):
    rows = stacked.shape[0] // 2
    lane = lax.broadcasted_iota(jnp.int32, (rows, stacked.shape[1]), 1)
    return jnp.where(lane < HD, stacked[:rows], stacked[rows:])


def attend_kernel(
    hidden, seg_col, seg_row, gain, offset, w_qkv, bias, w_out, part, normed, qkv, mixed, probs
):
    rows, width = hidden.shape
    half = w_qkv.shape[1] // 3

    @pl.loop(0, rows // ROWS)
    def _(i):
        at = pl.ds(pl.multiple_of(i * ROWS, ROWS), ROWS)
        xhat, _ = normalised(hidden[at, :].astype(F32))
        normed[at, :] = (xhat * gain[...] + offset[...]).astype(BF16)

    @pl.loop(0, 3)
    def _(i):
        at = pl.ds(pl.multiple_of(i * half, half), half)
        qkv[:, at] = (matmul(normed[...], w_qkv[:, at]) + bias[:, at]).astype(BF16)

    for i in range(rows // ROWS):
        at = slice(i * ROWS, (i + 1) * ROWS)
        seen = (i + 1) * ROWS
        query_at = i * ROWS + lax.broadcasted_iota(jnp.int32, (ROWS, seen), 0)
        key_at = lax.broadcasted_iota(jnp.int32, (ROWS, seen), 1)
        allowed = (key_at <= query_at) & (seg_col[at, :] == seg_row[:, :seen])
        penalty = jnp.where(allowed, 0.0, MASKED)
        penalty = jnp.concatenate([penalty, penalty], axis=0)
        for j in range(half // 128):
            q = split_heads(qkv[at, j * 128 : (j + 1) * 128] * jnp.bfloat16(HD**-0.5))
            k = qkv[:seen, half + j * 128 : half + (j + 1) * 128]
            v = qkv[:seen, 2 * half + j * 128 : 2 * half + (j + 1) * 128]
            scores = jnp.where(penalty == 0.0, matmul_t(q, k), MASKED)
            exps = jnp.exp(scores - jnp.max(scores, axis=-1, keepdims=True))
            p = (exps * (1.0 / jnp.sum(exps, axis=-1, keepdims=True))).astype(BF16)
            probs[j, i, :, :seen] = p
            mixed[at, j * 128 : (j + 1) * 128] = join_heads(matmul(p, v)).astype(BF16)

    @pl.loop(0, 2)
    def _(i):
        at = pl.ds(pl.multiple_of(i * 256, 256), 256)
        part[at, :] = matmul(mixed[at, :], w_out[...]).astype(BF16)


def attend(hidden, seg_col, seg_row, w):
    rows, width = hidden.shape
    half = w["qkv"].shape[1] // 3
    args = [hidden, seg_col, seg_row, w["ln1_gain"][None], w["ln1_bias"][None], w["qkv"], w["qkv_bias"][None], w["out"]]
    outs = [shape((rows, width), BF16)]
    kept = [shape((rows, width), BF16), shape((rows, 3 * half), BF16), shape((rows, half), BF16)]
    outs += kept + [shape((half // 128, rows // ROWS, 2 * ROWS, rows), BF16)]
    flops = 2 * rows * (width * 4 * half + 4 * rows * half)
    return call(attend_kernel, outs, [], args, flops)


def attend_back_kernel(
    own, other, grad, middle, gain, w_out, qkv, probs, w_qkv,
    g_middle, g_branch, g_qkv, part, sums, g_mixed, g_key, g_value
):
    rows, width = grad.shape
    half = w_qkv.shape[1] // 3
    scale = HD**-0.5
    sums[...] = jnp.zeros_like(sums)

    @pl.loop(0, rows // ROWS)
    def _(i):
        at = pl.ds(pl.multiple_of(i * ROWS, ROWS), ROWS)
        g_norm = own[at, :].astype(F32) + other[at, :].astype(F32)
        xhat, inverse = normalised(middle[at, :])
        value = grad[at, :].astype(F32) + norm_back(g_norm, xhat, inverse, gain[...])
        g_middle[at, :] = value
        branch = value.astype(BF16)
        g_branch[at, :] = branch
        sums[0:1, :] += jnp.sum(g_norm * xhat, axis=0, keepdims=True)
        sums[1:2, :] += jnp.sum(g_norm, axis=0, keepdims=True)
        sums[2:3, :] += jnp.sum(branch.astype(F32), axis=0, keepdims=True)

    g_mixed[...] = matmul_t(g_branch[...], w_out[...]).astype(BF16)

    for i in reversed(range(rows // ROWS)):
        at = slice(i * ROWS, (i + 1) * ROWS)
        seen = (i + 1) * ROWS
        for j in range(half // 128):
            lanes = slice(j * 128, (j + 1) * 128)
            q = split_heads(qkv[at, lanes] * jnp.bfloat16(scale))
            k = qkv[:seen, half + j * 128 : half + (j + 1) * 128] * jnp.bfloat16(scale)
            v = qkv[:seen, 2 * half + j * 128 : 2 * half + (j + 1) * 128]
            g = split_heads(g_mixed[at, lanes])
            p = probs[j, i, :, :seen]
            p_full = p.astype(F32)
            g_probs = matmul_t(g, v)
            inner = jnp.sum(p_full * g_probs, axis=-1, keepdims=True)
            g_scores = (p_full * (g_probs - inner)).astype(BF16)
            g_qkv[at, lanes] = join_heads(matmul(g_scores, k)).astype(BF16)
            key_term = t_matmul(g_scores, q)
            value_term = t_matmul(p, g)
            if seen == rows:
                g_key[:, lanes] = key_term
                g_value[:, lanes] = value_term
            else:
                g_key[:seen, lanes] += key_term
                g_value[:seen, lanes] += value_term
    g_qkv[:, half : 2 * half] = g_key[...].astype(BF16)
    g_qkv[:, 2 * half :] = g_value[...].astype(BF16)

    @pl.loop(0, 2)
    def _(i):
        at = pl.ds(pl.multiple_of(i * 256, 256), 256)
        part[at, :] = matmul_t(g_qkv[at, :], w_qkv[...]).astype(BF16)


def attend_back(own, other, grad, middle, qkv, probs, w):
    rows, width = grad.shape
    half = w["qkv"].shape[1] // 3
    args = [own, other, grad, middle, w["ln2_gain"][None], w["out"], qkv, probs, w["qkv"]]
    outs = [
        shape((rows, width), F32),
        shape((rows, width), BF16),
        shape((rows, 3 * half), BF16),
        shape((rows, width), BF16),
        shape((8, width), F32),
    ]
    scratch = [
        pltpu.VMEM((rows, half), BF16),
        pltpu.VMEM((rows, half), F32),
        pltpu.VMEM((rows, half), F32),
    ]
    flops = 2 * rows * (width * 4 * half + 8 * rows * half)
    return call(attend_back_kernel, outs, scratch, args, flops)


def feed_back_kernel(grad, *refs):
    slopes, ups, downs, (part,) = refs[0:2], refs[2:4], refs[4:6], refs[6:]
    half = grad.shape[0] // 2

    @pl.loop(0, 2)
    def _(i):
        at = pl.ds(pl.multiple_of(i * half, half), half)
        total = None
        for slope, up, down in zip(slopes, ups, downs):
            g = (matmul_t(grad[at, :], down[...]) * slope[at, :].astype(F32)).astype(BF16)
            term = matmul_t(g, up[...])
            total = term if total is None else total + term
        part[at, :] = total.astype(BF16)


def feed_back_rows(grad, slopes, w):
    args = [grad, *slopes, *w["up"], *w["down"]]
    flops = 8 * grad.size * w["up"][0].shape[1]
    return call(feed_back_kernel, [shape(grad.shape, BF16)], [], args, flops)[0]


def input_back(part, hidden, g_middle, w, core):
    rows = part.shape[0] // 2
    g_norm1 = part_of(part, core, rows).astype(F32) + between(part_of(part, 1 - core, rows)).astype(F32)
    xhat1, inv1 = normalised(part_of(hidden, core, rows).astype(F32))
    own_middle = part_of(g_middle, core, rows)
    return own_middle + norm_back(g_norm1, xhat1, inv1, w["ln1_gain"]), g_norm1, xhat1


def tied(value, *others):
    return lax.optimization_barrier((value,) + others)[0]


class Sums:
    HOPS = ([(0, 1), (3, 2)], [(1, 2), (2, 1)], [(1, 0), (2, 3)])

    def __init__(self, count):
        self.line = lax.axis_size("replica") == 4
        place = lax.axis_index("replica")
        self.outer = (place == 0) | (place == 3)
        self.values = {}
        self.results = {}
        self.last = None
        stages = 4 if self.line else 1
        self.events = sorted((p + s, -s, p) for p in range(count) for s in range(stages))

    def chained(self, value):
        if self.last is not None:
            value = tied(value, self.last)
        self.last = value
        return value

    def put(self, piece, sides, after):
        sides = [(mine, across(other.astype(BF16))) for mine, other in sides]
        self.values[piece] = (sides, after)

    def run(self, until=None):
        while self.events:
            _, stage, piece = self.events.pop(0)
            stage = -stage
            if stage == 0:
                sides, after = self.values[piece]
                totals = [mine.astype(F32) + self.chained(got).astype(F32) for mine, got in sides]
                totals = [total.astype(BF16) for total in totals]
                seen = totals[0]
                value = after(*totals)
                if not self.line:
                    self.results[piece] = lax.psum(value.astype(F32), "replica")
            else:
                value, got = self.values[piece]
                got = self.chained(got)
                if stage == 3:
                    self.results[piece] = jnp.where(self.outer, got, value).astype(F32)
                else:
                    value = (value.astype(F32) + got.astype(F32)).astype(BF16)
                seen = value
            if self.line and stage < 3:
                self.values[piece] = (value, lax.ppermute(value, "replica", self.HOPS[stage]))
            if until == (piece, stage):
                break
        return seen


def shards(
    inputs,
    segments,
    cotangent,
    ln1_gain,
    ln1_bias,
    qkv_weight,
    qv_bias,
    out_weight,
    out_bias,
    ln2_gain,
    ln2_bias,
    up_weight,
    up_bias,
    down_weight,
    down_bias,
):
    place = lax.axis_index("fsdp")
    chip, core = place // 2, place % 2
    is_first = lax.axis_index("section") == 0
    width = inputs.shape[-1]
    half = width // 2
    shard = width // 4
    hidden_units = up_weight.shape[-1]
    group = hidden_units // 4

    def both(rows):
        return joined(core, rows, between(rows))

    def entered(values):
        mine = pick(values, chip, 0)[0]
        other = across(pick(values, 1 - chip, 0)[0])
        pair = ordered(chip, mine, other)
        return ordered(core, pair, between(pair), 1).reshape(-1, width), other

    small = jnp.concatenate(
        [v[0] for v in (ln1_gain, ln1_bias, qv_bias, out_bias, ln2_gain, ln2_bias, up_bias, down_bias)]
    )
    pair = ordered(core, small, between(small))
    small = ordered(chip, pair, across(pair)).reshape(4, -1).astype(F32)
    sizes = [shard, shard, 2 * shard, shard, shard, shard, group, shard]
    vectors = []
    at = 0
    for size in sizes:
        vectors.append(small[:, at : at + size].reshape(-1))
        at += size
    hidden, first = entered(inputs)

    def rows_of(value, size):
        count = value.shape[1] // (2 * size)
        sides = [
            jnp.concatenate([part_of(value, 2 * i + place, size, 1) for i in range(count)], 1)
            for place in (core, 1 - core)
        ]
        return joined(core, sides[0], between(sides[1]))

    own_qkv = rows_of(qkv_weight[0], half)
    got_qkv = across(qkv_weight[0])
    qkv = joined(chip, own_qkv, rows_of(got_qkv, half))

    got_out = tied(across(tied(out_weight[0], first)), got_qkv)
    same = chip == core
    out = joined(
        core,
        jnp.where(same, out_weight[0], got_out),
        between(jnp.where(same, got_out, out_weight[0])),
    )

    own, other = (part_of(up_weight[0], place, 2 * group, 1) for place in (chip, 1 - chip))
    got_up = tied(across(tied(other, first)), got_out)
    got_other = tied(across(tied(own, got_qkv)), got_up)
    got_down = tied(across(tied(down_weight[0][: group // 2], got_out)), got_other)
    got_last = tied(across(tied(down_weight[0][group // 2 :], got_up)), got_down)
    own, other = rows_of(own, group), rows_of(other, group)
    up = [
        joined(chip, own, rows_of(got_up, group)),
        joined(chip, other, rows_of(got_other, group)),
    ]
    down = [down_weight[0], jnp.concatenate([got_down, got_last])]

    qv = vectors[2].reshape(2, 2, half)
    zeros = jnp.zeros((half,), F32)
    up_vector = pick(vectors[6].reshape(2, 2, group), core, 1)
    w = {
        "ln1_gain": vectors[0],
        "ln1_bias": vectors[1],
        "qkv": qkv,
        "qkv_bias": jnp.concatenate([pick(qv[0], core), zeros, pick(qv[1], core)]),
        "out": out,
        "out_bias": vectors[3],
        "ln2_gain": vectors[4],
        "ln2_bias": vectors[5],
        "up": up,
        "up_bias": [pick(up_vector, chip), pick(up_vector, 1 - chip)],
        "down": down,
        "down_bias": vectors[7],
    }
    segment = pick(segments, chip, 0)[0]

    def attention(rows):
        return attend(rows, segment[:, None], segment[None], w)

    result, _ = forward(hidden, attention, w, core)
    arrived = both(lax.ppermute(result, "section", [(0, 1)]))
    grad, _ = entered(tied(cotangent, result))
    hidden = jnp.where(is_first, hidden, arrived)
    result, state = forward(hidden, attention, w, core)
    middle, attn_state, (normed2, activated, slopes) = state
    normed1, qkv_rows, mixed, probs = attn_state

    part = feed_back_rows(grad, slopes, w)
    g_middle, _, _, part, _ = attend_back(part, between(part), grad, middle, qkv_rows, probs, w)
    g_input, _, _ = input_back(part, hidden, g_middle, w, core)

    def left(value):
        block = value.shape[0] // 2
        pair = ordered(core, part_of(value, core, block), between(part_of(value, 1 - core, block)))
        return ordered(chip, pick(pair, chip), across(pick(pair, 1 - chip)))[None, :, None]

    arrived = both(lax.ppermute(g_input.astype(BF16), "section", [(1, 0)]))
    acts = left(tied(result, g_input))
    grad = jnp.where(is_first, arrived, grad)

    sums = Sums(4)
    rows = hidden.shape[0]

    def sides(values):
        return tuple(part_of(values, place, half, 1) for place in (chip, 1 - chip))

    def swapped(value):
        return jnp.concatenate([part_of(value, core, shard), between(part_of(value, 1 - core, shard))])

    other = t_matmul(activated[1], grad).astype(BF16)
    sums.put(0, [(t_matmul(activated[0], grad), other)], lambda v: v)
    g_pre, part = feed_back(grad, slopes, w)
    stay, leave = sides(normed2)
    up_sides = [(t_matmul(stay, g_pre[i]), t_matmul(leave, g_pre[1 - i])) for i in range(2)]
    sums.put(1, up_sides, lambda a, b: jnp.concatenate([swapped(a), swapped(b)]))
    other = between(part)
    g_middle, g_branch, g_qkv, part, norm_sums = attend_back(part, other, grad, middle, qkv_rows, probs, w)

    stay, leave = (t_matmul(side, g_qkv) for side in sides(normed1))
    term = t_matmul(mixed, g_branch).astype(BF16)
    term = joined(core, part_of(term, core, shard), between(part_of(term, 1 - core, shard)))

    def folded(value):
        return jnp.concatenate([value[:, :half], value[:, half:]])

    sums.put(2, [(stay[:, :width], leave[:, :width])], swapped)
    stay = jnp.concatenate([stay[:, width:], folded(part_of(term, chip, shard)).astype(F32)], 1)
    leave = jnp.concatenate([leave[:, width:].astype(BF16), folded(part_of(term, 1 - chip, shard))], 1)
    part = tied(part, leave, sums.run((0, 0)))
    g_input, g_norm1, xhat1 = input_back(part, hidden, g_middle, w, core)

    def once(value):
        return jnp.where(core == 0, value, 0.0)

    def placed_half(value):
        return ordered(core, value, jnp.zeros_like(value))

    ones = jnp.ones((8, rows), BF16)

    def column_sums(values):
        return matmul(ones, values)[0]

    bias_sums = column_sums(g_qkv).reshape(3, half)
    qv_grad = jnp.concatenate([placed_half(bias_sums[0]), placed_half(bias_sums[2])])
    up_sums = ordered(chip, *(column_sums(g) for g in g_pre))
    up_bias_grad = ordered(core, up_sums, jnp.zeros_like(up_sums), 1)
    small_grads = [
        jnp.sum(g_norm1 * xhat1, axis=0),
        jnp.sum(g_norm1, axis=0),
        qv_grad,
        once(norm_sums[2]),
        once(norm_sums[0]),
        once(norm_sums[1]),
        up_bias_grad,
        once(column_sums(grad)),
    ]
    small_grads = jnp.concatenate([v.reshape(2, 2, -1) for v in small_grads], axis=-1)
    small_grads = pick(small_grads, core, 1) + between(pick(small_grads, 1 - core, 1))
    small_grads = small_grads.reshape(2, 3, width)
    def last_piece(value, vectors):
        return jnp.concatenate([jnp.concatenate([swapped(value[:, :half]), value[:, half:]], 1), vectors])

    sums.put(3, [(stay, leave), (pick(small_grads, chip), pick(small_grads, 1 - chip))], last_piece)
    grads_in = left(g_input.astype(BF16)).astype(F32)
    sums.run()
    done = sums.results
    down_grad = done[0]
    units = jnp.split(done[1], 4)
    up_grad = joined(chip, *(joined(core, units[2 * i], units[2 * i + 1], 1) for i in range(2)), 1)
    query_key, value_out, small_grads = done[2], done[3][: 2 * shard], done[3][2 * shard :].reshape(-1)
    qkv_grad = [
        joined(core, u[:shard], u[shard:], 1)
        for u in (query_key[:, :half], query_key[:, half:], value_out[:, :half])
    ]
    qkv_grad = jnp.concatenate(qkv_grad, 1)
    out_grad = jnp.concatenate([value_out[:shard, half:], value_out[shard:, half:]], 1)
    small_out = []
    at = 0
    for size in sizes:
        small_out.append(small_grads[None, at : at + size])
        at += size
    g_ln1g, g_ln1b, g_qv, g_outb, g_ln2g, g_ln2b, g_upb, g_downb = small_out
    return (
        acts,
        grads_in,
        g_ln1g,
        g_ln1b,
        qkv_grad[None],
        g_qv,
        out_grad[None],
        g_outb,
        g_ln2g,
        g_ln2b,
        up_grad[None],
        g_upb,
        down_grad[None],
        g_downb,
    )


def solution(mesh):
    rows = P(None, "replica", "fsdp", None)
    vector = P("section", "fsdp")
    matrix = P("section", "fsdp", None)
    layer = P("section", None, "replica", "fsdp", None)
    weights = (
        vector,
        vector,
        matrix,
        vector,
        matrix,
        vector,
        vector,
        vector,
        matrix,
        vector,
        matrix,
        vector,
    )
    return jax.shard_map(
        shards,
        mesh=mesh,
        in_specs=(rows, P(None, "replica", None), rows) + weights,
        out_specs=(layer, layer) + weights,
        check_vma=False,
    )
```

```python
import jax
import jax.numpy as jnp
from jax import lax
from jax.experimental import pallas as pl
from jax.experimental.pallas import tpu as pltpu
from jax.sharding import PartitionSpec as P

HEADS = 12
HD = 64
EPS = 1e-05
MASKED = -1e30
F32 = jnp.float32
BF16 = jnp.bfloat16
ROWS = 128


def across(value):
    return lax.ppermute(value, "fsdp", [(i, i ^ 2) for i in range(4)])


def between(value):
    return lax.ppermute(value, "fsdp", [(i, i ^ 1) for i in range(4)])


def ordered(place, own, other, axis=0):
    first = place == 0
    return jnp.stack([jnp.where(first, own, other), jnp.where(first, other, own)], axis)


def joined(place, own, other, axis=0):
    first = place == 0
    return jnp.concatenate([jnp.where(first, own, other), jnp.where(first, other, own)], axis)


def part_of(value, place, size, axis=0):
    return lax.dynamic_slice_in_dim(value, place * size, size, axis)


def pick(value, place, axis=0):
    return lax.dynamic_index_in_dim(value, place, axis, keepdims=False)


def matmul(left, right):
    return jnp.dot(left, right, preferred_element_type=F32)


def matmul_t(left, right):
    return lax.dot_general(left, right, (((1,), (1,)), ((), ())), preferred_element_type=F32)


def t_matmul(left, right):
    return lax.dot_general(left, right, (((0,), (0,)), ((), ())), preferred_element_type=F32)


def normalised(values):
    centred = values - jnp.mean(values, axis=-1, keepdims=True)
    inverse = lax.rsqrt(jnp.mean(centred * centred, axis=-1, keepdims=True) + EPS)
    return centred * inverse, inverse


def norm_back(grad, xhat, inverse, gain):
    scaled = grad * gain
    return inverse * (
        scaled
        - jnp.mean(scaled, axis=-1, keepdims=True)
        - xhat * jnp.mean(scaled * xhat, axis=-1, keepdims=True)
    )


def gelu_parts(u):
    a = 0.7978845608028654
    b = 0.044715
    t = jnp.tanh(a * (u + b * u * u * u))
    value = 0.5 * u * (1.0 + t)
    slope = 0.5 * (1.0 + t) + 0.5 * u * (1.0 - t * t) * a * (1.0 + 3.0 * b * u * u)
    return value, slope


def feed(middle, w):
    xhat, inverse = normalised(middle)
    normed = (xhat * w["ln2_gain"] + w["ln2_bias"]).astype(BF16)
    activated, slopes = [], []
    part = None
    for up, bias, down in zip(w["up"], w["up_bias"], w["down"]):
        value, slope = gelu_parts(matmul(normed, up) + bias)
        value, slope = lax.optimization_barrier((value.astype(BF16), slope.astype(BF16)))
        activated.append(value)
        slopes.append(slope)
        term = matmul(value, down)
        part = term if part is None else part + term
    return part, (normed, activated, slopes)


def forward(hidden, attention, w, core):
    part, *attn_state = attention(hidden)
    middle = hidden.astype(F32) + part.astype(F32) + between(part).astype(F32) + w["out_bias"]
    part, feed_state = feed(middle, w)
    rows = part.shape[0] // 2
    other = between(part_of(part, 1 - core, rows).astype(BF16))
    result = part_of(middle, core, rows) + part_of(part, core, rows) + other.astype(F32) + w["down_bias"]
    return result.astype(BF16), (middle, attn_state, feed_state)


def feed_back(grad, slopes, w):
    g_pre = []
    part = None
    for slope, up, down in zip(slopes, w["up"], w["down"]):
        g = (matmul_t(grad, down) * slope.astype(F32)).astype(BF16)
        g_pre.append(g)
        term = matmul_t(g, up)
        part = term if part is None else part + term
    return g_pre, part.astype(BF16)


def call(kernel, outs, scratch, args, flops, smem=()):
    spec = pl.BlockSpec(memory_space=pltpu.VMEM)
    moved = sum(a.size * a.dtype.itemsize for a in args)
    moved += sum(o.size * o.dtype.itemsize for o in outs)
    return pl.pallas_call(
        kernel,
        out_shape=tuple(outs),
        in_specs=[pl.BlockSpec(memory_space=pltpu.SMEM) if i in smem else spec for i in range(len(args))],
        out_specs=tuple(spec for _ in outs),
        scratch_shapes=scratch,
        compiler_params=pltpu.CompilerParams(vmem_limit_bytes=40 << 20),
        cost_estimate=pl.CostEstimate(flops=flops, bytes_accessed=moved, transcendentals=0),
    )(*args)


def shape(dims, kind):
    return jax.ShapeDtypeStruct(dims, kind)


def split_heads(pair):
    lane = lax.broadcasted_iota(jnp.int32, pair.shape, 1)
    zero = jnp.zeros_like(pair)
    return jnp.concatenate([jnp.where(lane < HD, pair, zero), jnp.where(lane < HD, zero, pair)], axis=0)


def join_heads(stacked):
    rows = stacked.shape[0] // 2
    lane = lax.broadcasted_iota(jnp.int32, (rows, stacked.shape[1]), 1)
    return jnp.where(lane < HD, stacked[:rows], stacked[rows:])


def attend_kernel(
    hidden, seg_col, seg_row, gain, offset, w_qkv, bias, w_out, part, normed, qkv, mixed, probs
):
    rows, width = hidden.shape
    half = w_qkv.shape[1] // 3

    @pl.loop(0, rows // ROWS)
    def _(i):
        at = pl.ds(pl.multiple_of(i * ROWS, ROWS), ROWS)
        xhat, _ = normalised(hidden[at, :].astype(F32))
        normed[at, :] = (xhat * gain[...] + offset[...]).astype(BF16)

    @pl.loop(0, 3)
    def _(i):
        at = pl.ds(pl.multiple_of(i * half, half), half)
        qkv[:, at] = (matmul(normed[...], w_qkv[:, at]) + bias[:, at]).astype(BF16)

    for i in range(rows // ROWS):
        at = slice(i * ROWS, (i + 1) * ROWS)
        seen = (i + 1) * ROWS
        query_at = i * ROWS + lax.broadcasted_iota(jnp.int32, (ROWS, seen), 0)
        key_at = lax.broadcasted_iota(jnp.int32, (ROWS, seen), 1)
        allowed = (key_at <= query_at) & (seg_col[at, :] == seg_row[:, :seen])
        penalty = jnp.where(allowed, 0.0, MASKED)
        penalty = jnp.concatenate([penalty, penalty], axis=0)
        for j in range(half // 128):
            q = split_heads(qkv[at, j * 128 : (j + 1) * 128] * jnp.bfloat16(HD**-0.5))
            k = qkv[:seen, half + j * 128 : half + (j + 1) * 128]
            v = qkv[:seen, 2 * half + j * 128 : 2 * half + (j + 1) * 128]
            scores = jnp.where(penalty == 0.0, matmul_t(q, k), MASKED)
            exps = jnp.exp(scores - jnp.max(scores, axis=-1, keepdims=True))
            p = (exps * (1.0 / jnp.sum(exps, axis=-1, keepdims=True))).astype(BF16)
            probs[j, i, :, :seen] = p
            mixed[at, j * 128 : (j + 1) * 128] = join_heads(matmul(p, v)).astype(BF16)

    @pl.loop(0, 2)
    def _(i):
        at = pl.ds(pl.multiple_of(i * 256, 256), 256)
        part[at, :] = matmul(mixed[at, :], w_out[...]).astype(BF16)


def attend(hidden, seg_col, seg_row, w):
    rows, width = hidden.shape
    half = w["qkv"].shape[1] // 3
    args = [hidden, seg_col, seg_row, w["ln1_gain"][None], w["ln1_bias"][None], w["qkv"], w["qkv_bias"][None], w["out"]]
    outs = [shape((rows, width), BF16)]
    kept = [shape((rows, width), BF16), shape((rows, 3 * half), BF16), shape((rows, half), BF16)]
    outs += kept + [shape((half // 128, rows // ROWS, 2 * ROWS, rows), BF16)]
    flops = 2 * rows * (width * 4 * half + 4 * rows * half)
    return call(attend_kernel, outs, [], args, flops)


def attend_back_kernel(
    own, other, grad, middle, gain, w_out, qkv, probs, w_qkv,
    g_middle, g_branch, g_qkv, part, sums, g_mixed, g_key, g_value
):
    rows, width = grad.shape
    half = w_qkv.shape[1] // 3
    scale = HD**-0.5
    sums[...] = jnp.zeros_like(sums)

    @pl.loop(0, rows // ROWS)
    def _(i):
        at = pl.ds(pl.multiple_of(i * ROWS, ROWS), ROWS)
        g_norm = own[at, :].astype(F32) + other[at, :].astype(F32)
        xhat, inverse = normalised(middle[at, :])
        value = grad[at, :].astype(F32) + norm_back(g_norm, xhat, inverse, gain[...])
        g_middle[at, :] = value
        branch = value.astype(BF16)
        g_branch[at, :] = branch
        sums[0:1, :] += jnp.sum(g_norm * xhat, axis=0, keepdims=True)
        sums[1:2, :] += jnp.sum(g_norm, axis=0, keepdims=True)
        sums[2:3, :] += jnp.sum(branch.astype(F32), axis=0, keepdims=True)

    g_mixed[...] = matmul_t(g_branch[...], w_out[...]).astype(BF16)

    for i in reversed(range(rows // ROWS)):
        at = slice(i * ROWS, (i + 1) * ROWS)
        seen = (i + 1) * ROWS
        for j in range(half // 128):
            lanes = slice(j * 128, (j + 1) * 128)
            q = split_heads(qkv[at, lanes] * jnp.bfloat16(scale))
            k = qkv[:seen, half + j * 128 : half + (j + 1) * 128] * jnp.bfloat16(scale)
            v = qkv[:seen, 2 * half + j * 128 : 2 * half + (j + 1) * 128]
            g = split_heads(g_mixed[at, lanes])
            p = probs[j, i, :, :seen]
            p_full = p.astype(F32)
            g_probs = matmul_t(g, v)
            inner = jnp.sum(p_full * g_probs, axis=-1, keepdims=True)
            g_scores = (p_full * (g_probs - inner)).astype(BF16)
            g_qkv[at, lanes] = join_heads(matmul(g_scores, k)).astype(BF16)
            key_term = t_matmul(g_scores, q)
            value_term = t_matmul(p, g)
            if seen == rows:
                g_key[:, lanes] = key_term
                g_value[:, lanes] = value_term
            else:
                g_key[:seen, lanes] += key_term
                g_value[:seen, lanes] += value_term
    g_qkv[:, half : 2 * half] = g_key[...].astype(BF16)
    g_qkv[:, 2 * half :] = g_value[...].astype(BF16)

    @pl.loop(0, 2)
    def _(i):
        at = pl.ds(pl.multiple_of(i * 256, 256), 256)
        part[at, :] = matmul_t(g_qkv[at, :], w_qkv[...]).astype(BF16)


def attend_back(own, other, grad, middle, qkv, probs, w):
    rows, width = grad.shape
    half = w["qkv"].shape[1] // 3
    args = [own, other, grad, middle, w["ln2_gain"][None], w["out"], qkv, probs, w["qkv"]]
    outs = [
        shape((rows, width), F32),
        shape((rows, width), BF16),
        shape((rows, 3 * half), BF16),
        shape((rows, width), BF16),
        shape((8, width), F32),
    ]
    scratch = [
        pltpu.VMEM((rows, half), BF16),
        pltpu.VMEM((rows, half), F32),
        pltpu.VMEM((rows, half), F32),
    ]
    flops = 2 * rows * (width * 4 * half + 8 * rows * half)
    return call(attend_back_kernel, outs, scratch, args, flops)


def feed_back_kernel(grad, *refs):
    slopes, ups, downs, (part,) = refs[0:2], refs[2:4], refs[4:6], refs[6:]
    half = grad.shape[0] // 2

    @pl.loop(0, 2)
    def _(i):
        at = pl.ds(pl.multiple_of(i * half, half), half)
        total = None
        for slope, up, down in zip(slopes, ups, downs):
            g = (matmul_t(grad[at, :], down[...]) * slope[at, :].astype(F32)).astype(BF16)
            term = matmul_t(g, up[...])
            total = term if total is None else total + term
        part[at, :] = total.astype(BF16)


def feed_back_rows(grad, slopes, w):
    args = [grad, *slopes, *w["up"], *w["down"]]
    flops = 8 * grad.size * w["up"][0].shape[1]
    return call(feed_back_kernel, [shape(grad.shape, BF16)], [], args, flops)[0]


def input_back(part, hidden, g_middle, w, core):
    rows = part.shape[0] // 2
    g_norm1 = part_of(part, core, rows).astype(F32) + between(part_of(part, 1 - core, rows)).astype(F32)
    xhat1, inv1 = normalised(part_of(hidden, core, rows).astype(F32))
    own_middle = part_of(g_middle, core, rows)
    return own_middle + norm_back(g_norm1, xhat1, inv1, w["ln1_gain"]), g_norm1, xhat1


def tied(value, *others):
    return lax.optimization_barrier((value,) + others)[0]


class Sums:
    HOPS = ([(0, 1), (3, 2)], [(1, 2), (2, 1)], [(1, 0), (2, 3)])

    def __init__(self, count):
        self.line = lax.axis_size("replica") == 4
        place = lax.axis_index("replica")
        self.outer = (place == 0) | (place == 3)
        self.values = {}
        self.results = {}
        self.last = None
        stages = 4 if self.line else 1
        self.events = sorted((p + s, -(s % 3), p, s) for p in range(count) for s in range(stages))

    def chained(self, value):
        if self.last is not None:
            value = tied(value, self.last)
        self.last = value
        return value

    def put(self, piece, sides, after):
        sides = [(mine, across(other.astype(BF16))) for mine, other in sides]
        self.values[piece] = (sides, after)

    def run(self, until=None):
        while self.events:
            _, _, piece, stage = self.events.pop(0)
            if stage == 0:
                sides, after = self.values[piece]
                totals = [mine.astype(F32) + self.chained(got).astype(F32) for mine, got in sides]
                totals = [total.astype(BF16) for total in totals]
                seen = totals[0]
                value = after(*totals)
                if not self.line:
                    self.results[piece] = lax.psum(value.astype(F32), "replica")
            else:
                value, got = self.values[piece]
                got = self.chained(got)
                if stage == 3:
                    self.results[piece] = jnp.where(self.outer, got, value).astype(F32)
                else:
                    value = (value.astype(F32) + got.astype(F32)).astype(BF16)
                seen = value
            if self.line and stage < 3:
                self.values[piece] = (value, lax.ppermute(value, "replica", self.HOPS[stage]))
            if until == (piece, stage):
                break
        return seen


def shards(
    inputs,
    segments,
    cotangent,
    ln1_gain,
    ln1_bias,
    qkv_weight,
    qv_bias,
    out_weight,
    out_bias,
    ln2_gain,
    ln2_bias,
    up_weight,
    up_bias,
    down_weight,
    down_bias,
):
    place = lax.axis_index("fsdp")
    chip, core = place // 2, place % 2
    is_first = lax.axis_index("section") == 0
    width = inputs.shape[-1]
    half = width // 2
    shard = width // 4
    hidden_units = up_weight.shape[-1]
    group = hidden_units // 4

    def both(rows):
        return joined(core, rows, between(rows))

    def entered(values):
        mine = pick(values, chip, 0)[0]
        other = across(pick(values, 1 - chip, 0)[0])
        pair = ordered(chip, mine, other)
        return ordered(core, pair, between(pair), 1).reshape(-1, width), other

    small = jnp.concatenate(
        [v[0] for v in (ln1_gain, ln1_bias, qv_bias, out_bias, ln2_gain, ln2_bias, up_bias, down_bias)]
    )
    pair = ordered(core, small, between(small))
    small = ordered(chip, pair, across(pair)).reshape(4, -1).astype(F32)
    sizes = [shard, shard, 2 * shard, shard, shard, shard, group, shard]
    vectors = []
    at = 0
    for size in sizes:
        vectors.append(small[:, at : at + size].reshape(-1))
        at += size
    hidden, first = entered(inputs)

    def rows_of(value, size):
        count = value.shape[1] // (2 * size)
        sides = [
            jnp.concatenate([part_of(value, 2 * i + place, size, 1) for i in range(count)], 1)
            for place in (core, 1 - core)
        ]
        return joined(core, sides[0], between(sides[1]))

    own_qkv = rows_of(qkv_weight[0], half)
    got_qkv = across(qkv_weight[0])
    qkv = joined(chip, own_qkv, rows_of(got_qkv, half))

    got_out = tied(across(tied(out_weight[0], pair)), got_qkv)
    same = chip == core
    out = joined(
        core,
        jnp.where(same, out_weight[0], got_out),
        between(jnp.where(same, got_out, out_weight[0])),
    )

    own, other = (part_of(up_weight[0], place, 2 * group, 1) for place in (chip, 1 - chip))
    got_up = tied(across(tied(other, pair)), got_out)
    got_other = tied(across(tied(own, got_qkv)), got_up)
    got_down = tied(across(tied(down_weight[0][: group // 2], got_out)), got_other)
    got_last = tied(across(tied(down_weight[0][group // 2 :], got_up)), got_down)
    own, other = rows_of(own, group), rows_of(other, group)
    up = [
        joined(chip, own, rows_of(got_up, group)),
        joined(chip, other, rows_of(got_other, group)),
    ]
    down = [down_weight[0], jnp.concatenate([got_down, got_last])]

    qv = vectors[2].reshape(2, 2, half)
    zeros = jnp.zeros((half,), F32)
    up_vector = pick(vectors[6].reshape(2, 2, group), core, 1)
    w = {
        "ln1_gain": vectors[0],
        "ln1_bias": vectors[1],
        "qkv": qkv,
        "qkv_bias": jnp.concatenate([pick(qv[0], core), zeros, pick(qv[1], core)]),
        "out": out,
        "out_bias": vectors[3],
        "ln2_gain": vectors[4],
        "ln2_bias": vectors[5],
        "up": up,
        "up_bias": [pick(up_vector, chip), pick(up_vector, 1 - chip)],
        "down": down,
        "down_bias": vectors[7],
    }
    segment = pick(segments, chip, 0)[0]

    def attention(rows):
        return attend(rows, segment[:, None], segment[None], w)

    result, _ = forward(hidden, attention, w, core)
    arrived = both(lax.ppermute(result, "section", [(0, 1)]))
    grad, _ = entered(tied(cotangent, result))
    hidden = jnp.where(is_first, hidden, arrived)
    result, state = forward(hidden, attention, w, core)
    middle, attn_state, (normed2, activated, slopes) = state
    normed1, qkv_rows, mixed, probs = attn_state

    part = feed_back_rows(grad, slopes, w)
    g_middle, _, _, part, _ = attend_back(part, between(part), grad, middle, qkv_rows, probs, w)
    g_input, _, _ = input_back(part, hidden, g_middle, w, core)

    def left(value):
        block = value.shape[0] // 2
        pair = ordered(core, part_of(value, core, block), between(part_of(value, 1 - core, block)))
        return ordered(chip, pick(pair, chip), across(pick(pair, 1 - chip)))[None, :, None]

    arrived = both(lax.ppermute(g_input.astype(BF16), "section", [(1, 0)]))
    acts = left(tied(result, g_input))
    grad = jnp.where(is_first, arrived, grad)

    sums = Sums(4)
    rows = hidden.shape[0]

    def sides(values):
        return tuple(part_of(values, place, half, 1) for place in (chip, 1 - chip))

    def swapped(value):
        return jnp.concatenate([part_of(value, core, shard), between(part_of(value, 1 - core, shard))])

    other = t_matmul(activated[1], grad).astype(BF16)
    sums.put(0, [(t_matmul(activated[0], grad), other)], lambda v: v)
    g_pre, part = feed_back(grad, slopes, w)
    stay, leave = sides(normed2)
    up_sides = [(t_matmul(stay, g_pre[i]), t_matmul(leave, g_pre[1 - i])) for i in range(2)]
    sums.put(1, up_sides, lambda a, b: jnp.concatenate([swapped(a), swapped(b)]))
    other = between(part)
    g_middle, g_branch, g_qkv, part, norm_sums = attend_back(part, other, grad, middle, qkv_rows, probs, w)

    stay, leave = (t_matmul(side, g_qkv) for side in sides(normed1))
    term = t_matmul(mixed, g_branch).astype(BF16)
    term = joined(core, part_of(term, core, shard), between(part_of(term, 1 - core, shard)))

    def folded(value):
        return jnp.concatenate([value[:, :half], value[:, half:]])

    sums.put(2, [(stay[:, :width], leave[:, :width])], swapped)
    stay = jnp.concatenate([stay[:, width:], folded(part_of(term, chip, shard)).astype(F32)], 1)
    leave = jnp.concatenate([leave[:, width:].astype(BF16), folded(part_of(term, 1 - chip, shard))], 1)
    part = tied(part, leave, sums.run((0, 0)))
    g_input, g_norm1, xhat1 = input_back(part, hidden, g_middle, w, core)

    def once(value):
        return jnp.where(core == 0, value, 0.0)

    def placed_half(value):
        return ordered(core, value, jnp.zeros_like(value))

    ones = jnp.ones((8, rows), BF16)

    def column_sums(values):
        return matmul(ones, values)[0]

    bias_sums = column_sums(g_qkv).reshape(3, half)
    qv_grad = jnp.concatenate([placed_half(bias_sums[0]), placed_half(bias_sums[2])])
    up_sums = ordered(chip, *(column_sums(g) for g in g_pre))
    up_bias_grad = ordered(core, up_sums, jnp.zeros_like(up_sums), 1)
    small_grads = [
        jnp.sum(g_norm1 * xhat1, axis=0),
        jnp.sum(g_norm1, axis=0),
        qv_grad,
        once(norm_sums[2]),
        once(norm_sums[0]),
        once(norm_sums[1]),
        up_bias_grad,
        once(column_sums(grad)),
    ]
    small_grads = jnp.concatenate([v.reshape(2, 2, -1) for v in small_grads], axis=-1)
    small_grads = pick(small_grads, core, 1) + between(pick(small_grads, 1 - core, 1))
    small_grads = small_grads.reshape(2, 3, width)
    def last_piece(value, vectors):
        return jnp.concatenate([jnp.concatenate([swapped(value[:, :half]), value[:, half:]], 1), vectors])

    sums.put(3, [(stay, leave), (pick(small_grads, chip), pick(small_grads, 1 - chip))], last_piece)
    grads_in = left(g_input.astype(BF16)).astype(F32)
    sums.run()
    done = sums.results
    down_grad = done[0]
    units = jnp.split(done[1], 4)
    up_grad = joined(chip, *(joined(core, units[2 * i], units[2 * i + 1], 1) for i in range(2)), 1)
    query_key, value_out, small_grads = done[2], done[3][: 2 * shard], done[3][2 * shard :].reshape(-1)
    qkv_grad = [
        joined(core, u[:shard], u[shard:], 1)
        for u in (query_key[:, :half], query_key[:, half:], value_out[:, :half])
    ]
    qkv_grad = jnp.concatenate(qkv_grad, 1)
    out_grad = jnp.concatenate([value_out[:shard, half:], value_out[shard:, half:]], 1)
    small_out = []
    at = 0
    for size in sizes:
        small_out.append(small_grads[None, at : at + size])
        at += size
    g_ln1g, g_ln1b, g_qv, g_outb, g_ln2g, g_ln2b, g_upb, g_downb = small_out
    return (
        acts,
        grads_in,
        g_ln1g,
        g_ln1b,
        qkv_grad[None],
        g_qv,
        out_grad[None],
        g_outb,
        g_ln2g,
        g_ln2b,
        up_grad[None],
        g_upb,
        down_grad[None],
        g_downb,
    )


def solution(mesh):
    rows = P(None, "replica", "fsdp", None)
    vector = P("section", "fsdp")
    matrix = P("section", "fsdp", None)
    layer = P("section", None, "replica", "fsdp", None)
    weights = (
        vector,
        vector,
        matrix,
        vector,
        matrix,
        vector,
        vector,
        vector,
        matrix,
        vector,
        matrix,
        vector,
    )
    return jax.shard_map(
        shards,
        mesh=mesh,
        in_specs=(rows, P(None, "replica", None), rows) + weights,
        out_specs=(layer, layer) + weights,
        check_vma=False,
    )
```

```python
import jax
import jax.numpy as jnp
from jax import lax
from jax.experimental import pallas as pl
from jax.experimental.pallas import tpu as pltpu
from jax.sharding import PartitionSpec as P

HEADS = 12
HD = 64
EPS = 1e-05
MASKED = -1e30
F32 = jnp.float32
BF16 = jnp.bfloat16
ROWS = 128


def across(value):
    return lax.ppermute(value, "fsdp", [(i, i ^ 2) for i in range(4)])


def between(value):
    return lax.ppermute(value, "fsdp", [(i, i ^ 1) for i in range(4)])


def ordered(place, own, other, axis=0):
    first = place == 0
    return jnp.stack([jnp.where(first, own, other), jnp.where(first, other, own)], axis)


def joined(place, own, other, axis=0):
    first = place == 0
    return jnp.concatenate([jnp.where(first, own, other), jnp.where(first, other, own)], axis)


def part_of(value, place, size, axis=0):
    return lax.dynamic_slice_in_dim(value, place * size, size, axis)


def pick(value, place, axis=0):
    return lax.dynamic_index_in_dim(value, place, axis, keepdims=False)


def matmul(left, right):
    return jnp.dot(left, right, preferred_element_type=F32)


def matmul_t(left, right):
    return lax.dot_general(left, right, (((1,), (1,)), ((), ())), preferred_element_type=F32)


def t_matmul(left, right):
    return lax.dot_general(left, right, (((0,), (0,)), ((), ())), preferred_element_type=F32)


def normalised(values):
    centred = values - jnp.mean(values, axis=-1, keepdims=True)
    inverse = lax.rsqrt(jnp.mean(centred * centred, axis=-1, keepdims=True) + EPS)
    return centred * inverse, inverse


def norm_back(grad, xhat, inverse, gain):
    scaled = grad * gain
    return inverse * (
        scaled
        - jnp.mean(scaled, axis=-1, keepdims=True)
        - xhat * jnp.mean(scaled * xhat, axis=-1, keepdims=True)
    )


def gelu_parts(u):
    a = 0.7978845608028654
    b = 0.044715
    t = jnp.tanh(a * (u + b * u * u * u))
    value = 0.5 * u * (1.0 + t)
    slope = 0.5 * (1.0 + t) + 0.5 * u * (1.0 - t * t) * a * (1.0 + 3.0 * b * u * u)
    return value, slope


def feed(middle, w):
    xhat, inverse = normalised(middle)
    normed = (xhat * w["ln2_gain"] + w["ln2_bias"]).astype(BF16)
    activated, slopes = [], []
    part = None
    for up, bias, down in zip(w["up"], w["up_bias"], w["down"]):
        value, slope = gelu_parts(matmul(normed, up) + bias)
        value, slope = lax.optimization_barrier((value.astype(BF16), slope.astype(BF16)))
        activated.append(value)
        slopes.append(slope)
        term = matmul(value, down)
        part = term if part is None else part + term
    return part, (normed, activated, slopes)


def forward(hidden, attention, w, core):
    part, *attn_state = attention(hidden)
    middle = hidden.astype(F32) + part.astype(F32) + between(part).astype(F32) + w["out_bias"]
    part, feed_state = feed(middle, w)
    rows = part.shape[0] // 2
    other = between(part_of(part, 1 - core, rows).astype(BF16))
    result = part_of(middle, core, rows) + part_of(part, core, rows) + other.astype(F32) + w["down_bias"]
    return result.astype(BF16), (middle, attn_state, feed_state)


def feed_back(grad, slopes, w):
    g_pre = []
    part = None
    for slope, up, down in zip(slopes, w["up"], w["down"]):
        g = (matmul_t(grad, down) * slope.astype(F32)).astype(BF16)
        g_pre.append(g)
        term = matmul_t(g, up)
        part = term if part is None else part + term
    return g_pre, part.astype(BF16)


def call(kernel, outs, scratch, args, flops, smem=()):
    spec = pl.BlockSpec(memory_space=pltpu.VMEM)
    moved = sum(a.size * a.dtype.itemsize for a in args)
    moved += sum(o.size * o.dtype.itemsize for o in outs)
    return pl.pallas_call(
        kernel,
        out_shape=tuple(outs),
        in_specs=[pl.BlockSpec(memory_space=pltpu.SMEM) if i in smem else spec for i in range(len(args))],
        out_specs=tuple(spec for _ in outs),
        scratch_shapes=scratch,
        compiler_params=pltpu.CompilerParams(vmem_limit_bytes=40 << 20),
        cost_estimate=pl.CostEstimate(flops=flops, bytes_accessed=moved, transcendentals=0),
    )(*args)


def shape(dims, kind):
    return jax.ShapeDtypeStruct(dims, kind)


def split_heads(pair):
    lane = lax.broadcasted_iota(jnp.int32, pair.shape, 1)
    zero = jnp.zeros_like(pair)
    return jnp.concatenate([jnp.where(lane < HD, pair, zero), jnp.where(lane < HD, zero, pair)], axis=0)


def join_heads(stacked):
    rows = stacked.shape[0] // 2
    lane = lax.broadcasted_iota(jnp.int32, (rows, stacked.shape[1]), 1)
    return jnp.where(lane < HD, stacked[:rows], stacked[rows:])


def attend_kernel(
    hidden, seg_col, seg_row, gain, offset, w_qkv, bias, w_out, part, normed, qkv, mixed, probs
):
    rows, width = hidden.shape
    half = w_qkv.shape[1] // 3

    @pl.loop(0, rows // ROWS)
    def _(i):
        at = pl.ds(pl.multiple_of(i * ROWS, ROWS), ROWS)
        xhat, _ = normalised(hidden[at, :].astype(F32))
        normed[at, :] = (xhat * gain[...] + offset[...]).astype(BF16)

    @pl.loop(0, 3)
    def _(i):
        at = pl.ds(pl.multiple_of(i * half, half), half)
        qkv[:, at] = (matmul(normed[...], w_qkv[:, at]) + bias[:, at]).astype(BF16)

    for i in range(rows // ROWS):
        at = slice(i * ROWS, (i + 1) * ROWS)
        seen = (i + 1) * ROWS
        query_at = i * ROWS + lax.broadcasted_iota(jnp.int32, (ROWS, seen), 0)
        key_at = lax.broadcasted_iota(jnp.int32, (ROWS, seen), 1)
        allowed = (key_at <= query_at) & (seg_col[at, :] == seg_row[:, :seen])
        penalty = jnp.where(allowed, 0.0, MASKED)
        penalty = jnp.concatenate([penalty, penalty], axis=0)
        for j in range(half // 128):
            q = split_heads(qkv[at, j * 128 : (j + 1) * 128] * jnp.bfloat16(HD**-0.5))
            k = qkv[:seen, half + j * 128 : half + (j + 1) * 128]
            v = qkv[:seen, 2 * half + j * 128 : 2 * half + (j + 1) * 128]
            scores = jnp.where(penalty == 0.0, matmul_t(q, k), MASKED)
            exps = jnp.exp(scores - jnp.max(scores, axis=-1, keepdims=True))
            p = (exps * (1.0 / jnp.sum(exps, axis=-1, keepdims=True))).astype(BF16)
            probs[j, i, :, :seen] = p
            mixed[at, j * 128 : (j + 1) * 128] = join_heads(matmul(p, v)).astype(BF16)

    @pl.loop(0, 2)
    def _(i):
        at = pl.ds(pl.multiple_of(i * 256, 256), 256)
        part[at, :] = matmul(mixed[at, :], w_out[...]).astype(BF16)


def attend(hidden, seg_col, seg_row, w):
    rows, width = hidden.shape
    half = w["qkv"].shape[1] // 3
    args = [hidden, seg_col, seg_row, w["ln1_gain"][None], w["ln1_bias"][None], w["qkv"], w["qkv_bias"][None], w["out"]]
    outs = [shape((rows, width), BF16)]
    kept = [shape((rows, width), BF16), shape((rows, 3 * half), BF16), shape((rows, half), BF16)]
    outs += kept + [shape((half // 128, rows // ROWS, 2 * ROWS, rows), BF16)]
    flops = 2 * rows * (width * 4 * half + 4 * rows * half)
    return call(attend_kernel, outs, [], args, flops)


def attend_back_kernel(
    own, other, grad, middle, gain, w_out, qkv, probs, w_qkv,
    g_middle, g_branch, g_qkv, part, sums, g_mixed, g_key, g_value
):
    rows, width = grad.shape
    half = w_qkv.shape[1] // 3
    scale = HD**-0.5
    sums[...] = jnp.zeros_like(sums)

    @pl.loop(0, rows // ROWS)
    def _(i):
        at = pl.ds(pl.multiple_of(i * ROWS, ROWS), ROWS)
        g_norm = own[at, :].astype(F32) + other[at, :].astype(F32)
        xhat, inverse = normalised(middle[at, :])
        value = grad[at, :].astype(F32) + norm_back(g_norm, xhat, inverse, gain[...])
        g_middle[at, :] = value
        branch = value.astype(BF16)
        g_branch[at, :] = branch
        sums[0:1, :] += jnp.sum(g_norm * xhat, axis=0, keepdims=True)
        sums[1:2, :] += jnp.sum(g_norm, axis=0, keepdims=True)
        sums[2:3, :] += jnp.sum(branch.astype(F32), axis=0, keepdims=True)

    g_mixed[...] = matmul_t(g_branch[...], w_out[...]).astype(BF16)

    for i in reversed(range(rows // ROWS)):
        at = slice(i * ROWS, (i + 1) * ROWS)
        seen = (i + 1) * ROWS
        for j in range(half // 128):
            lanes = slice(j * 128, (j + 1) * 128)
            q = split_heads(qkv[at, lanes] * jnp.bfloat16(scale))
            k = qkv[:seen, half + j * 128 : half + (j + 1) * 128] * jnp.bfloat16(scale)
            v = qkv[:seen, 2 * half + j * 128 : 2 * half + (j + 1) * 128]
            g = split_heads(g_mixed[at, lanes])
            p = probs[j, i, :, :seen]
            p_full = p.astype(F32)
            g_probs = matmul_t(g, v)
            inner = jnp.sum(p_full * g_probs, axis=-1, keepdims=True)
            g_scores = (p_full * (g_probs - inner)).astype(BF16)
            g_qkv[at, lanes] = join_heads(matmul(g_scores, k)).astype(BF16)
            key_term = t_matmul(g_scores, q)
            value_term = t_matmul(p, g)
            if seen == rows:
                g_key[:, lanes] = key_term
                g_value[:, lanes] = value_term
            else:
                g_key[:seen, lanes] += key_term
                g_value[:seen, lanes] += value_term
    g_qkv[:, half : 2 * half] = g_key[...].astype(BF16)
    g_qkv[:, 2 * half :] = g_value[...].astype(BF16)

    @pl.loop(0, 2)
    def _(i):
        at = pl.ds(pl.multiple_of(i * 256, 256), 256)
        part[at, :] = matmul_t(g_qkv[at, :], w_qkv[...]).astype(BF16)


def attend_back(own, other, grad, middle, qkv, probs, w):
    rows, width = grad.shape
    half = w["qkv"].shape[1] // 3
    args = [own, other, grad, middle, w["ln2_gain"][None], w["out"], qkv, probs, w["qkv"]]
    outs = [
        shape((rows, width), F32),
        shape((rows, width), BF16),
        shape((rows, 3 * half), BF16),
        shape((rows, width), BF16),
        shape((8, width), F32),
    ]
    scratch = [
        pltpu.VMEM((rows, half), BF16),
        pltpu.VMEM((rows, half), F32),
        pltpu.VMEM((rows, half), F32),
    ]
    flops = 2 * rows * (width * 4 * half + 8 * rows * half)
    return call(attend_back_kernel, outs, scratch, args, flops)


def feed_back_kernel(grad, *refs):
    slopes, ups, downs, (part,) = refs[0:2], refs[2:4], refs[4:6], refs[6:]
    half = grad.shape[0] // 2

    @pl.loop(0, 2)
    def _(i):
        at = pl.ds(pl.multiple_of(i * half, half), half)
        total = None
        for slope, up, down in zip(slopes, ups, downs):
            g = (matmul_t(grad[at, :], down[...]) * slope[at, :].astype(F32)).astype(BF16)
            term = matmul_t(g, up[...])
            total = term if total is None else total + term
        part[at, :] = total.astype(BF16)


def feed_back_rows(grad, slopes, w):
    args = [grad, *slopes, *w["up"], *w["down"]]
    flops = 8 * grad.size * w["up"][0].shape[1]
    return call(feed_back_kernel, [shape(grad.shape, BF16)], [], args, flops)[0]


def input_back(part, hidden, g_middle, w, core):
    rows = part.shape[0] // 2
    g_norm1 = part_of(part, core, rows).astype(F32) + between(part_of(part, 1 - core, rows)).astype(F32)
    xhat1, inv1 = normalised(part_of(hidden, core, rows).astype(F32))
    own_middle = part_of(g_middle, core, rows)
    return own_middle + norm_back(g_norm1, xhat1, inv1, w["ln1_gain"]), g_norm1, xhat1


def tied(value, *others):
    return lax.optimization_barrier((value,) + others)[0]


class Sums:
    HOPS = ([(0, 1), (3, 2)], [(1, 2), (2, 1)], [(1, 0), (2, 3)])

    def __init__(self, count):
        self.line = lax.axis_size("replica") == 4
        place = lax.axis_index("replica")
        self.outer = (place == 0) | (place == 3)
        self.values = {}
        self.results = {}
        self.last = None
        stages = 4 if self.line else 1
        self.events = sorted((p + s, -(s % 3), p, s) for p in range(count) for s in range(stages))

    def chained(self, value):
        if self.last is not None:
            value = tied(value, self.last)
        self.last = value
        return value

    def put(self, piece, sides, after):
        sides = [(mine, across(other.astype(BF16))) for mine, other in sides]
        self.values[piece] = (sides, after)

    def run(self, until=None):
        while self.events:
            _, _, piece, stage = self.events.pop(0)
            if stage == 0:
                sides, after = self.values[piece]
                totals = [mine.astype(F32) + self.chained(got).astype(F32) for mine, got in sides]
                totals = [total.astype(BF16) for total in totals]
                seen = totals[0]
                value = after(*totals)
                if not self.line:
                    self.results[piece] = lax.psum(value.astype(F32), "replica")
            else:
                value, got = self.values[piece]
                got = self.chained(got)
                if stage == 3:
                    self.results[piece] = jnp.where(self.outer, got, value).astype(F32)
                else:
                    value = (value.astype(F32) + got.astype(F32)).astype(BF16)
                seen = value
            if self.line and stage < 3:
                self.values[piece] = (value, lax.ppermute(value, "replica", self.HOPS[stage]))
            if until == (piece, stage):
                break
        return seen


def shards(
    inputs,
    segments,
    cotangent,
    ln1_gain,
    ln1_bias,
    qkv_weight,
    qv_bias,
    out_weight,
    out_bias,
    ln2_gain,
    ln2_bias,
    up_weight,
    up_bias,
    down_weight,
    down_bias,
):
    place = lax.axis_index("fsdp")
    chip, core = place // 2, place % 2
    is_first = lax.axis_index("section") == 0
    width = inputs.shape[-1]
    half = width // 2
    shard = width // 4
    hidden_units = up_weight.shape[-1]
    group = hidden_units // 4

    def both(rows):
        return joined(core, rows, between(rows))

    def entered(values):
        mine = pick(values, chip, 0)[0]
        other = across(pick(values, 1 - chip, 0)[0])
        pair = ordered(chip, mine, other)
        return ordered(core, pair, between(pair), 1).reshape(-1, width), other

    small = jnp.concatenate(
        [v[0] for v in (ln1_gain, ln1_bias, qv_bias, out_bias, ln2_gain, ln2_bias, up_bias, down_bias)]
    )
    pair = ordered(core, small, between(small))
    small = ordered(chip, pair, across(pair)).reshape(4, -1).astype(F32)
    sizes = [shard, shard, 2 * shard, shard, shard, shard, group, shard]
    vectors = []
    at = 0
    for size in sizes:
        vectors.append(small[:, at : at + size].reshape(-1))
        at += size
    hidden, first = entered(inputs)

    def rows_of(value, size):
        count = value.shape[1] // (2 * size)
        sides = [
            jnp.concatenate([part_of(value, 2 * i + place, size, 1) for i in range(count)], 1)
            for place in (core, 1 - core)
        ]
        return joined(core, sides[0], between(sides[1]))

    own_qkv = rows_of(qkv_weight[0], half)
    got_qkv = across(qkv_weight[0])
    qkv = joined(chip, own_qkv, rows_of(got_qkv, half))

    got_out = tied(across(tied(out_weight[0], pair)), got_qkv)
    same = chip == core
    out = joined(
        core,
        jnp.where(same, out_weight[0], got_out),
        between(jnp.where(same, got_out, out_weight[0])),
    )

    own, other = (part_of(up_weight[0], place, 2 * group, 1) for place in (chip, 1 - chip))
    got_up = tied(across(tied(other, pair)), got_out)
    got_other = tied(across(tied(own, got_qkv)), got_up)
    got_down = tied(across(tied(down_weight[0][: group // 2], got_out)), got_other)
    got_last = tied(across(tied(down_weight[0][group // 2 :], got_up)), got_down)
    own, other = rows_of(own, group), rows_of(other, group)
    up = [
        joined(chip, own, rows_of(got_up, group)),
        joined(chip, other, rows_of(got_other, group)),
    ]
    down = [down_weight[0], jnp.concatenate([got_down, got_last])]

    qv = vectors[2].reshape(2, 2, half)
    zeros = jnp.zeros((half,), F32)
    up_vector = pick(vectors[6].reshape(2, 2, group), core, 1)
    w = {
        "ln1_gain": vectors[0],
        "ln1_bias": vectors[1],
        "qkv": qkv,
        "qkv_bias": jnp.concatenate([pick(qv[0], core), zeros, pick(qv[1], core)]),
        "out": out,
        "out_bias": vectors[3],
        "ln2_gain": vectors[4],
        "ln2_bias": vectors[5],
        "up": up,
        "up_bias": [pick(up_vector, chip), pick(up_vector, 1 - chip)],
        "down": down,
        "down_bias": vectors[7],
    }
    segment = pick(segments, chip, 0)[0]

    def attention(rows):
        return attend(rows, segment[:, None], segment[None], w)

    result, _ = forward(hidden, attention, w, core)
    arrived = both(lax.ppermute(result, "section", [(0, 1)]))
    grad, _ = entered(tied(cotangent, result))
    hidden = jnp.where(is_first, hidden, arrived)
    result, state = forward(hidden, attention, w, core)
    middle, attn_state, (normed2, activated, slopes) = state
    normed1, qkv_rows, mixed, probs = attn_state

    part = feed_back_rows(grad, slopes, w)
    g_middle, _, _, part, _ = attend_back(part, between(part), grad, middle, qkv_rows, probs, w)
    g_input, _, _ = input_back(part, hidden, g_middle, w, core)

    def left(value):
        block = value.shape[0] // 2
        pair = ordered(core, part_of(value, core, block), between(part_of(value, 1 - core, block)))
        return ordered(chip, pick(pair, chip), across(pick(pair, 1 - chip)))[None, :, None]

    arrived = both(lax.ppermute(g_input.astype(BF16), "section", [(1, 0)]))
    acts = left(tied(result, g_input))
    grad = jnp.where(is_first, arrived, grad)

    sums = Sums(4)
    rows = hidden.shape[0]

    def sides(values):
        return tuple(part_of(values, place, half, 1) for place in (chip, 1 - chip))

    def swapped(value):
        return jnp.concatenate([part_of(value, core, shard), between(part_of(value, 1 - core, shard))])

    other = t_matmul(activated[1], grad).astype(BF16)
    sums.put(0, [(t_matmul(activated[0], grad), other)], lambda v: v)
    g_pre, part = feed_back(tied(grad, other), slopes, w)
    stay, leave = sides(normed2)
    up_sides = [(t_matmul(stay, g_pre[i]), t_matmul(leave, g_pre[1 - i])) for i in range(2)]
    sums.put(1, up_sides, lambda a, b: jnp.concatenate([swapped(a), swapped(b)]))
    other = between(part)
    g_middle, g_branch, g_qkv, part, norm_sums = attend_back(part, other, grad, middle, qkv_rows, probs, w)

    stay, leave = (t_matmul(side, g_qkv) for side in sides(normed1))
    term = t_matmul(mixed, g_branch).astype(BF16)
    term = joined(core, part_of(term, core, shard), between(part_of(term, 1 - core, shard)))

    def folded(value):
        return jnp.concatenate([value[:, :half], value[:, half:]])

    sums.put(2, [(stay[:, :width], leave[:, :width])], swapped)
    stay = jnp.concatenate([stay[:, width:], folded(part_of(term, chip, shard)).astype(F32)], 1)
    leave = jnp.concatenate([leave[:, width:].astype(BF16), folded(part_of(term, 1 - chip, shard))], 1)
    part = tied(part, leave, sums.run((0, 0)))
    g_input, g_norm1, xhat1 = input_back(part, hidden, g_middle, w, core)

    def once(value):
        return jnp.where(core == 0, value, 0.0)

    def placed_half(value):
        return ordered(core, value, jnp.zeros_like(value))

    ones = jnp.ones((8, rows), BF16)

    def column_sums(values):
        return matmul(ones, values)[0]

    bias_sums = column_sums(g_qkv).reshape(3, half)
    qv_grad = jnp.concatenate([placed_half(bias_sums[0]), placed_half(bias_sums[2])])
    up_sums = ordered(chip, *(column_sums(g) for g in g_pre))
    up_bias_grad = ordered(core, up_sums, jnp.zeros_like(up_sums), 1)
    small_grads = [
        jnp.sum(g_norm1 * xhat1, axis=0),
        jnp.sum(g_norm1, axis=0),
        qv_grad,
        once(norm_sums[2]),
        once(norm_sums[0]),
        once(norm_sums[1]),
        up_bias_grad,
        once(column_sums(grad)),
    ]
    small_grads = jnp.concatenate([v.reshape(2, 2, -1) for v in small_grads], axis=-1)
    small_grads = pick(small_grads, core, 1) + between(pick(small_grads, 1 - core, 1))
    small_grads = small_grads.reshape(2, 3, width)
    def last_piece(value, vectors):
        return jnp.concatenate([jnp.concatenate([swapped(value[:, :half]), value[:, half:]], 1), vectors])

    sums.put(3, [(stay, leave), (pick(small_grads, chip), pick(small_grads, 1 - chip))], last_piece)
    grads_in = left(g_input.astype(BF16)).astype(F32)
    sums.run()
    done = sums.results
    down_grad = done[0]
    units = jnp.split(done[1], 4)
    up_grad = joined(chip, *(joined(core, units[2 * i], units[2 * i + 1], 1) for i in range(2)), 1)
    query_key, value_out, small_grads = done[2], done[3][: 2 * shard], done[3][2 * shard :].reshape(-1)
    qkv_grad = [
        joined(core, u[:shard], u[shard:], 1)
        for u in (query_key[:, :half], query_key[:, half:], value_out[:, :half])
    ]
    qkv_grad = jnp.concatenate(qkv_grad, 1)
    out_grad = jnp.concatenate([value_out[:shard, half:], value_out[shard:, half:]], 1)
    small_out = []
    at = 0
    for size in sizes:
        small_out.append(small_grads[None, at : at + size])
        at += size
    g_ln1g, g_ln1b, g_qv, g_outb, g_ln2g, g_ln2b, g_upb, g_downb = small_out
    return (
        acts,
        grads_in,
        g_ln1g,
        g_ln1b,
        qkv_grad[None],
        g_qv,
        out_grad[None],
        g_outb,
        g_ln2g,
        g_ln2b,
        up_grad[None],
        g_upb,
        down_grad[None],
        g_downb,
    )


def solution(mesh):
    rows = P(None, "replica", "fsdp", None)
    vector = P("section", "fsdp")
    matrix = P("section", "fsdp", None)
    layer = P("section", None, "replica", "fsdp", None)
    weights = (
        vector,
        vector,
        matrix,
        vector,
        matrix,
        vector,
        vector,
        vector,
        matrix,
        vector,
        matrix,
        vector,
    )
    return jax.shard_map(
        shards,
        mesh=mesh,
        in_specs=(rows, P(None, "replica", None), rows) + weights,
        out_specs=(layer, layer) + weights,
        check_vma=False,
    )
```
